512 devices in a mesh: rows: 64 (over y, z_lo, core), maps: 8 (over z_hi, x).
Axes of the slice: x: 4, y: 4, z: 16 (z_hi: 2, z_lo: 8; z = z_hi * 8 + z_lo), core: 2. Of those that a mesh axis runs over, the one named last changes fastest.
Arguments:
- counts: int32 [8, 1024, 32768], P(None, 'rows', 'maps'), may hold values from 0 to 2999, as said below
- weights: float32 [8], replicated, may hold values from 0.2 to 5
Outputs:
- barycenter: float32 [1024, 32768], P('rows', 'maps')
The draws below stay inside these ranges and needn't reach their ends.
Inputs may be any that keep to these rules, and one draw needn't show every extreme that they name: `counts`: each count is drawn evenly below a ceiling that grows with the row from 1000 (first row) to 3000 (last row), times a level of 1 to 4 over 4 that is drawn for each run of 64 columns; the largest count, 2999, is reached in every draw.
All inputs are finite; a program needn't handle non-finite values.
Results may differ from the reference program's by a relative error of at most 0.0001.
Values sent between devices are 32-bit elements; how exact they have to be, the bound alone decides.
No kernel may reach another device: no remote copies, remote signals or barrier semaphores. Data moves between devices by JAX's collectives and lax.ppermute only.
A program may use at most 64 MiB of HBM per device.

```python
import math
import jax
import jax.numpy as jnp
from jax import lax

MAPS = 8
WIDTH = 32768
HALF = 8
ITERS = 2
HEIGHT = 1024


def draw_counts(key, part):
    level_key = jax.random.fold_in(key, 17)
    point_key = jax.random.fold_in(key, 29)
    row_index = lax.broadcasted_iota(jnp.int32, (MAPS, HEIGHT, WIDTH), 1)
    ceiling = 1000 + 2000 * row_index // (HEIGHT - 1)
    levels = jax.random.randint(level_key, (MAPS, HEIGHT, WIDTH // 64), 1, 5)
    levels = jnp.repeat(levels, 64, axis=2)
    upper = ceiling * levels // 4
    raw_counts = jax.random.randint(point_key, (MAPS, HEIGHT, WIDTH), 0, upper)
    return raw_counts.at[0, HEIGHT - 1, 0].set(2999).astype(jnp.int32)


def setup_inputs(seed: int = 0) -> dict:
    splits = jax.random.split(jax.random.key(seed), 3)
    counts = draw_counts(jax.random.fold_in(splits[2], 71), 0)
    weights = jnp.clip(jnp.exp(jax.random.uniform(splits[1], (MAPS,), jnp.float32, math.log(0.2), math.log(5.0))), 0.2, 5.0)
    return dict(counts=counts, weights=weights)


def kernel_vector():
    spread = 0.45 * HALF
    across = jnp.arange(-HALF, HALF + 1).astype(jnp.float32)
    shape_taps = jnp.exp(-across * across / (2.0 * spread * spread))
    return shape_taps / jnp.sum(shape_taps)


def smooth_axis(grid_field, kernel_taps, direction):
    padding = [(0, 0), (0, 0)]
    padding[direction] = (HALF, HALF)
    padded = jnp.pad(grid_field, padding)
    length = grid_field.shape[direction]
    result = jnp.zeros(grid_field.shape, jnp.float32)
    for offset in range(2 * HALF + 1):
        result = result + kernel_taps[offset] * lax.slice_in_dim(padded, offset, offset + length, axis=direction)
    return result


def smooth_map(grid_field):
    kernel_taps = kernel_vector()
    return smooth_axis(smooth_axis(grid_field, kernel_taps, 0), kernel_taps, 1)


def reference(counts, weights):
    smoothed = counts.astype(jnp.float32) + 1.0
    totals = jnp.sum(smoothed, axis=(1, 2))
    cell_count = float(HEIGHT * WIDTH)
    density = smoothed * (cell_count / totals)[:, None, None]
    mixing = weights / jnp.sum(weights)
    scaling = jnp.ones(density.shape, jnp.float32)
    barycenter = jnp.zeros((HEIGHT, WIDTH), jnp.float32)
    for iteration in range(ITERS):
        forward = lax.map(smooth_map, scaling)
        dual_scale = density / forward
        marginal = scaling * lax.map(smooth_map, dual_scale)
        barycenter = jnp.exp(jnp.sum(mixing[:, None, None] * jnp.log(marginal), axis=0))
        if iteration + 1 < ITERS:
            scaling = scaling * barycenter[None] / marginal
    return barycenter
```

```python
import functools

import jax
import jax.numpy as jnp
import numpy as np
from jax import lax
from jax.experimental import pallas as pl
from jax.experimental.pallas import tpu as pltpu
from jax.sharding import PartitionSpec as P

HALF = 8
K = 8
LANES = 128
EDGE = -1

SPLIT_A, SPLIT_B = 14, 24
CHUNKS = (
    (31,) + tuple(range(SPLIT_A)),
    tuple(range(SPLIT_A, SPLIT_B)),
    tuple(range(SPLIT_B, 31)),
)
READS = (
    tuple(range(SPLIT_A)),
    tuple(range(SPLIT_A - 2, SPLIT_B)),
    tuple(range(SPLIT_B - 2, 32)) + (EDGE, 0, 1, 2),
)


def taps():
    spread = 0.45 * HALF
    a = np.arange(-HALF, HALF + 1, dtype=np.float64)
    g = np.exp(-a * a / (2.0 * spread * spread))
    return g / g.sum()


def band(out_pos, in_pos):
    g = taps()
    d = np.asarray(in_pos)[None, :] - np.asarray(out_pos)[:, None]
    return np.where(np.abs(d) <= HALF, g[np.clip(d + HALF, 0, 2 * HALF)], 0.0)


def split_np(x):
    x = np.asarray(x, np.float32)
    hi = x.astype(jnp.bfloat16)
    lo = (x - hi.astype(np.float32)).astype(jnp.bfloat16)
    return hi, lo


def positions(core):
    own = np.arange(16)
    if core == 0:
        zo, zq, q, f = np.arange(-24, -16), np.arange(-16, 0), np.arange(16, 32), np.arange(32, 40)
        z8, q8 = np.arange(-8, 0), np.arange(16, 24)
    else:
        zo, zq, q, f = np.arange(32, 40), np.arange(16, 32), np.arange(-16, 0), np.arange(-24, -16)
        z8, q8 = np.arange(16, 24), np.arange(-8, 0)
    return np.concatenate([zo, zq, own, q, f]), np.concatenate([zq, own, q]), np.concatenate([z8, own, q8]), own


def matrices():
    out = []
    for s in range(3):
        both = [split_np(band(positions(c)[s + 1], positions(c)[s])) for c in (0, 1)]
        out += [np.stack([b[0] for b in both]), np.stack([b[1] for b in both])]
    cols = band(np.arange(256), np.arange(512) - 128).T
    return out + list(split_np(cols))


def split(x):
    hi = x.astype(jnp.bfloat16)
    lo = (x - hi.astype(jnp.float32)).astype(jnp.bfloat16)
    return hi, lo


def dot(a, b):
    return jnp.dot(a, b, preferred_element_type=jnp.float32)


def dot3(ah, al, bh, bl):
    return dot(ah, bh) + (dot(al, bh) + dot(ah, bl))


def window_sum(pos, size):
    g = taps()
    total = jnp.zeros(pos.shape, jnp.float32)
    for i, a in enumerate(range(-HALF, HALF + 1)):
        total = total + jnp.where((pos + a >= 0) & (pos + a < size), np.float32(g[i]), np.float32(0.0))
    return total


def kernel(reads, sources, height, width, scal, mix, relcol, *refs):
    n_in = 1 + 4 * len(sources) + (2 if EDGE in reads else 0)
    zo = refs[0]
    parts = {c: refs[1 + 4 * i : 5 + 4 * i] for i, c in enumerate(sources)}
    halo = refs[1 + 4 * len(sources) : n_in]
    g1h, g1l, g2h, g2l, g3h, g3l, bh, bl = refs[n_in : n_in + 8]
    out = refs[n_in + 8]
    n_ref, rr, rc, cv, h1h, h1l, h2h, h2l, h3h, h3l, u_ref, w_ref = refs[n_in + 9 :]
    blocks = len(reads)
    tiles = blocks // 2
    core, outer, row0, col0 = scal[0], scal[1], scal[2], scal[3]
    foff = pl.multiple_of(core * 8, 8)

    where = {b: (c, i) for c, ids in enumerate(CHUNKS) for i, b in enumerate(ids)}
    at = 0
    while at < blocks:
        dst = pl.ds(at * LANES, LANES)
        if reads[at] == EDGE:
            lane = lax.broadcasted_iota(jnp.int32, (K, 8, LANES), 2)
            left, right = halo
            for r in range(0, 56, 8):
                n_ref[:, r : r + 8, dst] = jnp.where(lane < 64, right[:, r : r + 8, :], left[:, r : r + 8, :])
            fr = pl.ds(56 + foff, 8)
            n_ref[:, 56:64, dst] = jnp.where(lane < 64, right[:, fr, :], left[:, fr, :])
            at += 1
            continue
        c, i = where[reads[at]]
        run = 1
        while at + run < blocks and where.get(reads[at + run]) == (c, i + run) and reads[at + run] == reads[at] + run:
            run += 1
        own, q, zq, f = parts[c]
        dst = pl.ds(at * LANES, run * LANES)
        src = pl.ds(i * LANES, run * LANES)
        n_ref[:, 0:8, dst] = zo[:, :, pl.ds(reads[at] * LANES, run * LANES)]
        n_ref[:, 8:24, dst] = zq[:, :, src]
        n_ref[:, 24:40, dst] = own[:, :, src]
        n_ref[:, 40:56, dst] = q[:, :, src]
        n_ref[:, 56:64, dst] = f[:, pl.ds(foff, 8), src]
        at += run

    i = lax.broadcasted_iota(jnp.int32, (64, 256), 0)
    flipped = jnp.where(i < 8, i + 32, jnp.where(i < 24, i + 8, jnp.where(i < 40, i - 24, jnp.where(i < 56, i - 56, i - 80))))
    row = row0 + jnp.where(core == 0, i - 24, flipped)
    total = window_sum(row, height)
    rr[...] = jnp.where(total > 0.0, 1.0 / jnp.where(total > 0.0, total, 1.0), 0.0)
    col = col0 + relcol[...]
    total = window_sum(col, width)
    rc[...] = jnp.where(total > 0.0, 1.0 / jnp.where(total > 0.0, total, 1.0), 0.0)
    cv[...] = jnp.where((col >= 0) & (col < width), 1.0, 0.0)

    for ref in (h1h, h1l, h2h, h2l, h3h, h3l):
        rows = ref.shape[0]
        ref[:, 0:LANES] = jnp.zeros((rows, LANES), jnp.bfloat16)
        ref[:, pl.ds((blocks + 1) * LANES, LANES)] = jnp.zeros((rows, LANES), jnp.bfloat16)

    def tile(j):
        return pl.ds(pl.multiple_of(j * 256, 256), 256)

    def inner(j):
        return pl.ds(pl.multiple_of(j * 256 + LANES, LANES), 256)

    def wide(j):
        return pl.ds(pl.multiple_of(j * 256, 256), 512)

    g1 = (g1h[core], g1l[core])
    g2 = (g2h[core], g2l[core])
    g3 = (g3h[core], g3l[core])

    @pl.loop(0, tiles)
    def _(j):
        scale = rr[...] * rc[0:1, tile(j)]
        for k in range(K):
            dh, dl = split(n_ref[k, :, tile(j)] * scale)
            hh, hl = split(dot3(*g1, dh, dl))
            h1h[48 * k : 48 * k + 48, inner(j)] = hh
            h1l[48 * k : 48 * k + 48, inner(j)] = hl

    @pl.loop(0, tiles)
    def _(j):
        u_ref[...] = dot3(h1h[:, wide(j)], h1l[:, wide(j)], bh[...], bl[...])
        acc = jnp.zeros((48, 256), jnp.float32)
        for k in range(K):
            acc = acc + mix[k] * jnp.log(u_ref[48 * k : 48 * k + 48, :])
        valid = cv[0:1, tile(j)] > 0.0
        index = lax.broadcasted_iota(jnp.int32, (48, 256), 0)
        valid = valid & ((index >= 16) | (outer == 0))
        geo = jnp.exp(acc)
        for k in range(K):
            w = jnp.where(valid, geo / u_ref[48 * k : 48 * k + 48, :], 0.0)
            w_ref[k, :, tile(j)] = w[16:32]
            wh, wl = split(w)
            hh, hl = split(dot3(*g2, wh, wl))
            h2h[32 * k : 32 * k + 32, inner(j)] = hh
            h2l[32 * k : 32 * k + 32, inner(j)] = hl

    zrow = pl.ds(pl.multiple_of(jnp.where(core == 0, 16, 8), 8), 8)
    qrow = pl.ds(pl.multiple_of(jnp.where(core == 0, 40, 48), 8), 8)

    @pl.loop(0, tiles)
    def _(j):
        u_ref[0 : 32 * K, :] = dot3(h2h[:, wide(j)], h2l[:, wide(j)], bh[...], bl[...])
        valid = cv[0:1, tile(j)] > 0.0
        for k in range(K):
            n = jnp.concatenate([n_ref[k, zrow, tile(j)], n_ref[k, 24:40, tile(j)], n_ref[k, qrow, tile(j)]], axis=0)
            d = jnp.where(valid, n / u_ref[32 * k : 32 * k + 32, :], 0.0)
            dh, dl = split(d)
            hh, hl = split(dot3(*g3, dh, dl))
            h3h[16 * k : 16 * k + 16, inner(j)] = hh
            h3l[16 * k : 16 * k + 16, inner(j)] = hl

    @pl.loop(0, tiles)
    def _(j):
        u_ref[0 : 16 * K, :] = dot3(h3h[:, wide(j)], h3l[:, wide(j)], bh[...], bl[...])
        acc = jnp.zeros((16, 256), jnp.float32)
        for k in range(K):
            acc = acc + mix[k] * jnp.log(w_ref[k, :, tile(j)] * u_ref[16 * k : 16 * k + 16, :])
        out[:, tile(j)] = acc


def relative_columns(reads):
    lane = np.arange(LANES)
    cols = [np.where(lane < 64, 4096 + lane, lane - LANES) if b == EDGE else b * LANES + lane for b in reads]
    return np.tile(np.concatenate(cols).astype(np.int32)[None], (8, 1))


def run_kernel(which, sources, height, width, scal, mix, arrays):
    reads = READS[which]
    blocks = len(reads)
    lanes = blocks * LANES
    wide = (blocks + 2) * LANES
    consts = matrices()
    smem = pl.BlockSpec(memory_space=pltpu.SMEM)
    vmem = pl.BlockSpec(memory_space=pltpu.VMEM)
    scratch = [
        pltpu.VMEM((K, 64, lanes), jnp.float32),
        pltpu.VMEM((64, 256), jnp.float32),
        pltpu.VMEM((8, lanes), jnp.float32),
        pltpu.VMEM((8, lanes), jnp.float32),
    ]
    for rows in (48, 32, 16):
        scratch += [pltpu.VMEM((rows * K, wide), jnp.bfloat16)] * 2
    scratch += [pltpu.VMEM((48 * K, 256), jnp.float32), pltpu.VMEM((K, 16, lanes), jnp.float32)]
    return pl.pallas_call(
        functools.partial(kernel, reads, sources, height, width),
        out_shape=jax.ShapeDtypeStruct((16, lanes), jnp.float32),
        in_specs=[smem, smem] + [vmem] * (1 + len(arrays) + len(consts)),
        out_specs=vmem,
        scratch_shapes=scratch,
        name=f"barycenter_{which}",
    )(scal, mix, jnp.asarray(relative_columns(reads)), *arrays, *[jnp.asarray(c) for c in consts])


def blocks_of(x, ids):
    runs, start = [], 0
    for i in range(1, len(ids) + 1):
        if i == len(ids) or ids[i] != ids[i - 1] + 1:
            runs.append(x[..., ids[start] * LANES : (ids[i - 1] + 1) * LANES])
            start = i
    return runs[0] if len(runs) == 1 else jnp.concatenate(runs, axis=-1)


def on_device(counts, weights):
    n_rows, n_cols = lax.axis_size("rows"), lax.axis_size("maps")
    height, width = n_rows * counts.shape[1], n_cols * counts.shape[2]
    r, m = lax.axis_index("rows"), lax.axis_index("maps")
    core = r % 2
    outer = ((r == 0) | (r == n_rows - 1)).astype(jnp.int32)
    scal = jnp.stack([core, outer, r * counts.shape[1], m * counts.shape[2]]).astype(jnp.int32)
    mix = weights / jnp.sum(weights)

    swap = [(i, i ^ 1) for i in range(n_rows)]
    hop = [(i, i + 2) for i in range(0, n_rows - 2, 2)] + [(i, i - 2) for i in range(3, n_rows, 2)]
    to_right = [(i, i + 1) for i in range(n_cols - 1)]
    to_left = [(i + 1, i) for i in range(n_cols - 1)]

    n = counts.astype(jnp.float32) + 1.0
    zo = lax.ppermute(jnp.where(core == 0, n[:, 8:], n[:, :8]), "rows", hop)
    own = [blocks_of(n, ids) for ids in CHUNKS]
    q = [lax.ppermute(x, "rows", swap) for x in own]
    zq = [lax.ppermute(x, "rows", hop) for x in q]
    f = [lax.ppermute(x, "rows", swap) for x in zq]

    sums = jnp.sum(n, axis=(1, 2))
    for axis, size in (("rows", n_rows), ("maps", n_cols)):
        bit = 1
        while bit < size:
            sums = sums + lax.ppermute(sums, axis, [(i, i ^ bit) for i in range(size)])
            bit *= 2
    log_scale = jnp.sum(mix * jnp.log(float(height * width) / sums))

    def column(b):
        i = CHUNKS[0].index(b)
        cols = slice(i * LANES, (i + 1) * LANES)
        return jnp.concatenate(
            [zo[..., b * LANES : (b + 1) * LANES]] + [x[0][..., cols] for x in (zq, own, q, f)], axis=1
        )

    left = lax.ppermute(column(31), "maps", to_right)
    right = lax.ppermute(column(0), "maps", to_left)

    outs = []
    for which, sources in enumerate(((0,), (0, 1), (0, 1, 2))):
        arrays = [zo]
        for c in sources:
            arrays += [own[c], q[c], zq[c], f[c]]
        if EDGE in READS[which]:
            arrays += [left, right]
        outs.append(run_kernel(which, sources, height, width, scal, mix, arrays))
    last = 32 - (SPLIT_B - 2)
    pieces = [
        outs[2][:, (last + 1) * LANES : (last + 2) * LANES],
        outs[0][:, LANES : (SPLIT_A - 1) * LANES],
        outs[1][:, LANES : -LANES],
        outs[2][:, LANES : last * LANES],
    ]
    return jnp.exp(jnp.concatenate(pieces, axis=1) + log_scale)


def solution(mesh):
    return jax.shard_map(
        on_device, mesh=mesh, in_specs=(P(None, "rows", "maps"), P()), out_specs=P("rows", "maps"), check_vma=False
    )
```

```python
import functools

import jax
import jax.numpy as jnp
import numpy as np
from jax import lax
from jax.experimental import pallas as pl
from jax.experimental.pallas import tpu as pltpu
from jax.sharding import PartitionSpec as P


HALF = 8
K = 8
LANES = 128
EDGE = -1

FIRST, SECOND = 12, 23
CHUNKS = (
    (29, 30, 31) + tuple(range(FIRST)),
    tuple(range(FIRST, SECOND)),
    tuple(range(SECOND, 29)),
)
KERNELS = (
    (tuple(range(FIRST)), (0,)),
    ((29, 30, 31, EDGE, 0, 1), (0,)),
    (tuple(range(FIRST - 3, SECOND)), (0, 1)),
    (tuple(range(SECOND - 2, 31)), (0, 1, 2)),
)
KEPT = (
    ((1, FIRST - 2),),
    ((30, 31), (0, 0)),
    ((FIRST - 1, SECOND - 2),),
    ((SECOND - 1, 29),),
)


def taps():
    spread = 0.45 * HALF
    a = np.arange(-HALF, HALF + 1, dtype=np.float64)
    g = np.exp(-a * a / (2.0 * spread * spread))
    return g / g.sum()


def band(out_pos, in_pos):
    g = taps()
    d = np.asarray(in_pos)[None, :] - np.asarray(out_pos)[:, None]
    return np.where(np.abs(d) <= HALF, g[np.clip(d + HALF, 0, 2 * HALF)], 0.0)


def split_np(x):
    x = np.asarray(x, np.float32)
    hi = x.astype(jnp.bfloat16)
    lo = (x - hi.astype(np.float32)).astype(jnp.bfloat16)
    return hi, lo


def positions(core):
    own = np.arange(16)
    if core == 0:
        zo, zq, q, f = np.arange(-24, -16), np.arange(-16, 0), np.arange(16, 32), np.arange(32, 40)
        z8, q8 = np.arange(-8, 0), np.arange(16, 24)
    else:
        zo, zq, q, f = np.arange(32, 40), np.arange(16, 32), np.arange(-16, 0), np.arange(-24, -16)
        z8, q8 = np.arange(16, 24), np.arange(-8, 0)
    return np.concatenate([zo, zq, own, q, f]), np.concatenate([zq, own, q]), np.concatenate([z8, own, q8]), own


def matrices():
    out = []
    for s in range(3):
        both = [split_np(band(positions(c)[s + 1], positions(c)[s])) for c in (0, 1)]
        out.append(np.stack([np.concatenate([h, l, h], axis=1) for h, l in both]))
    near = split_np(band(np.arange(256), np.arange(256)).T)
    lane = np.arange(LANES)
    far = split_np(band(np.arange(256), np.where(lane < 64, 256 + lane, lane - LANES)).T)
    out.append(np.concatenate([near[0], near[0], near[1], far[0], far[0], far[1]], axis=0))
    return out


def split(x):
    hi = x.astype(jnp.bfloat16)
    lo = (x - hi.astype(jnp.float32)).astype(jnp.bfloat16)
    return hi, lo


def dot(a, b):
    return jnp.dot(a, b, preferred_element_type=jnp.float32)


def row_pass(g, x):
    hi, lo = split(x)
    return split(dot(g, jnp.concatenate([hi, hi, lo], axis=0)))


def window_sum(pos, size):
    g = taps()
    total = jnp.zeros(pos.shape, jnp.float32)
    for i, a in enumerate(range(-HALF, HALF + 1)):
        total = total + jnp.where((pos + a >= 0) & (pos + a < size), np.float32(g[i]), np.float32(0.0))
    return total


def copies(reads, foff, zo, parts, n_ref):
    where = {b: (c, i) for c, ids in enumerate(CHUNKS) for i, b in enumerate(ids)}
    out = []
    at = 0
    while at < len(reads):
        if reads[at] == EDGE:
            at += 1
            continue
        c, i = where[reads[at]]
        run = 1
        while at + run < len(reads) and reads[at + run] == reads[at] + run and where[reads[at + run]] == (c, i + run):
            run += 1
        own, q, zq, f = parts[c]
        dst = pl.ds(at * LANES, run * LANES)
        src = pl.ds(i * LANES, run * LANES)
        out += [
            (zo.at[:, :, pl.ds(reads[at] * LANES, run * LANES)], n_ref.at[:, pl.ds(0, 8), dst]),
            (zq.at[:, :, src], n_ref.at[:, pl.ds(8, 16), dst]),
            (own.at[:, :, src], n_ref.at[:, pl.ds(24, 16), dst]),
            (q.at[:, :, src], n_ref.at[:, pl.ds(40, 16), dst]),
            (f.at[:, pl.ds(foff, 8), src], n_ref.at[:, pl.ds(56, 8), dst]),
        ]
        at += run
    return out


def count_copies(reads, sources):
    class Fake:
        at = property(lambda self: self)

        def __getitem__(self, _):
            return self

    x = Fake()
    return len(copies(reads, 0, x, {c: (x,) * 4 for c in sources}, x))


def kernel(reads, sources, joins, height, width, scal, mix, relcol, *refs):
    n_in = 1 + 4 * len(sources) + (2 if EDGE in reads else 0)
    zo = refs[0]
    parts = {c: refs[1 + 4 * i : 5 + 4 * i] for i, c in enumerate(sources)}
    halo = refs[1 + 4 * len(sources) : n_in]
    g1, g2, g3, bm = refs[n_in : n_in + 4]
    n_in += 4
    if joins:
        log_scale, earlier = refs[n_in], refs[n_in + 1 : n_in + len(joins)]
        n_in += len(joins)
    out = refs[n_in]
    n_ref, rr, rc, cv, h1h, h1l, h2h, h2l, h3h, h3l, u_ref, w_ref, sems = refs[n_in + 1 :][:13]
    acc_ref = refs[-1] if joins else out
    blocks = len(reads)
    tiles = blocks // 2
    core, outer, row0, col0 = scal[0], scal[1], scal[2], scal[3]
    foff = pl.multiple_of(core * 8, 8)

    moves = [
        pltpu.make_async_copy(src, dst, sems.at[i])
        for i, (src, dst) in enumerate(copies(reads, foff, zo, parts, n_ref))
    ]
    for move in moves:
        move.start()

    i = lax.broadcasted_iota(jnp.int32, (64, 256), 0)
    flipped = jnp.where(i < 8, i + 32, jnp.where(i < 24, i + 8, jnp.where(i < 40, i - 24, jnp.where(i < 56, i - 56, i - 80))))
    row = row0 + jnp.where(core == 0, i - 24, flipped)
    total = window_sum(row, height)
    rr[...] = jnp.where(total > 0.0, 1.0 / jnp.where(total > 0.0, total, 1.0), 0.0)
    col = col0 + relcol[...]
    total = window_sum(col, width)
    rc[...] = jnp.where(total > 0.0, 1.0 / jnp.where(total > 0.0, total, 1.0), 0.0)
    cv[...] = jnp.where((col >= 0) & (col < width), 1.0, 0.0)

    for ref in (h1h, h1l, h2h, h2l, h3h, h3l):
        rows = ref.shape[0]
        ref[:, 0:LANES] = jnp.zeros((rows, LANES), jnp.bfloat16)
        ref[:, pl.ds((blocks + 1) * LANES, LANES)] = jnp.zeros((rows, LANES), jnp.bfloat16)

    if EDGE in reads:
        dst = pl.ds(reads.index(EDGE) * LANES, LANES)
        lane = lax.broadcasted_iota(jnp.int32, (K, 8, LANES), 2)
        left, right = halo
        for r in range(0, 56, 8):
            n_ref[:, r : r + 8, dst] = jnp.where(lane < 64, right[:, r : r + 8, :], left[:, r : r + 8, :])
        fr = pl.ds(56 + foff, 8)
        n_ref[:, 56:64, dst] = jnp.where(lane < 64, right[:, fr, :], left[:, fr, :])

    for move in moves:
        move.wait()

    def tile(j):
        return pl.ds(pl.multiple_of(j * 256, 256), 256)

    def at(j, shift, size):
        return pl.ds(pl.multiple_of(j * 256 + shift, LANES), size)

    def column_pass(high, low, j):
        rows = high.shape[0]
        first = lax.broadcasted_iota(jnp.int32, (rows, LANES), 1) < 64
        mh, ml = high[:, at(j, LANES, 256)], low[:, at(j, LANES, 256)]
        eh = jnp.where(first, high[:, at(j, 3 * LANES, LANES)], high[:, at(j, 0, LANES)])
        el = jnp.where(first, low[:, at(j, 3 * LANES, LANES)], low[:, at(j, 0, LANES)])
        return dot(jnp.concatenate([mh, ml, mh, eh, el, eh], axis=1), bm[...])

    @pl.loop(0, tiles)
    def _(j):
        scale = rr[...] * rc[0:1, tile(j)]
        for k in range(K):
            hh, hl = row_pass(g1[core], n_ref[k, :, tile(j)] * scale)
            h1h[48 * k : 48 * k + 48, at(j, LANES, 256)] = hh
            h1l[48 * k : 48 * k + 48, at(j, LANES, 256)] = hl

    @pl.loop(0, tiles)
    def _(j):
        u_ref[...] = column_pass(h1h, h1l, j)
        acc = jnp.zeros((48, 256), jnp.float32)
        for k in range(K):
            acc = acc + mix[k] * jnp.log(u_ref[48 * k : 48 * k + 48, :])
        valid = cv[0:1, tile(j)] > 0.0
        index = lax.broadcasted_iota(jnp.int32, (48, 256), 0)
        valid = valid & ((index >= 16) | (outer == 0))
        geo = jnp.exp(acc)
        for k in range(K):
            w = jnp.where(valid, geo / u_ref[48 * k : 48 * k + 48, :], 0.0)
            w_ref[k, :, tile(j)] = w[16:32]
            hh, hl = row_pass(g2[core], w)
            h2h[32 * k : 32 * k + 32, at(j, LANES, 256)] = hh
            h2l[32 * k : 32 * k + 32, at(j, LANES, 256)] = hl

    zrow = pl.ds(pl.multiple_of(jnp.where(core == 0, 16, 8), 8), 8)
    qrow = pl.ds(pl.multiple_of(jnp.where(core == 0, 40, 48), 8), 8)

    @pl.loop(0, tiles)
    def _(j):
        u_ref[0 : 32 * K, :] = column_pass(h2h, h2l, j)
        valid = cv[0:1, tile(j)] > 0.0
        for k in range(K):
            n = jnp.concatenate([n_ref[k, zrow, tile(j)], n_ref[k, 24:40, tile(j)], n_ref[k, qrow, tile(j)]], axis=0)
            d = jnp.where(valid, n / u_ref[32 * k : 32 * k + 32, :], 0.0)
            hh, hl = row_pass(g3[core], d)
            h3h[16 * k : 16 * k + 16, at(j, LANES, 256)] = hh
            h3l[16 * k : 16 * k + 16, at(j, LANES, 256)] = hl

    @pl.loop(0, tiles)
    def _(j):
        u_ref[0 : 16 * K, :] = column_pass(h3h, h3l, j)
        acc = jnp.zeros((16, 256), jnp.float32)
        for k in range(K):
            acc = acc + mix[k] * jnp.log(w_ref[k, :, tile(j)] * u_ref[16 * k : 16 * k + 16, :])
        acc_ref[:, tile(j)] = acc

    for i, moved in enumerate(joins):
        ref = acc_ref if i == len(joins) - 1 else earlier[i]
        for src, dst, count in moved:
            piece = ref[:, src * LANES : (src + count) * LANES] + log_scale[0]
            out[:, dst * LANES : (dst + count) * LANES] = jnp.exp(piece)


def relative_columns(reads):
    lane = np.arange(LANES)
    cols = [np.where(lane < 64, 4096 + lane, lane - LANES) if b == EDGE else b * LANES + lane for b in reads]
    return np.tile(np.concatenate(cols).astype(np.int32)[None], (8, 1))


def run_kernel(which, height, width, scal, mix, arrays, earlier, log_scale):
    reads, sources = KERNELS[which]
    blocks = len(reads)
    lanes = blocks * LANES
    wide = (blocks + 2) * LANES
    consts = matrices()
    smem = pl.BlockSpec(memory_space=pltpu.SMEM)
    vmem = pl.BlockSpec(memory_space=pltpu.VMEM)
    anywhere = pl.BlockSpec(memory_space=pl.ANY)
    halos = 2 if EDGE in reads else 0
    scratch = [
        pltpu.VMEM((K, 64, lanes), jnp.float32),
        pltpu.VMEM((64, 256), jnp.float32),
        pltpu.VMEM((8, lanes), jnp.float32),
        pltpu.VMEM((8, lanes), jnp.float32),
    ]
    for rows in (48, 32, 16):
        scratch += [pltpu.VMEM((rows * K, wide), jnp.bfloat16)] * 2
    scratch += [
        pltpu.VMEM((48 * K, 256), jnp.float32),
        pltpu.VMEM((K, 16, lanes), jnp.float32),
        pltpu.SemaphoreType.DMA((count_copies(reads, sources),)),
    ]
    in_specs = [smem, smem, vmem] + [anywhere] * (len(arrays) - halos) + [vmem] * (halos + len(consts))
    args = [scal, mix, jnp.asarray(relative_columns(reads)), *arrays, *[jnp.asarray(c) for c in consts]]
    joins = ()
    if earlier:
        joins = tuple(
            tuple((KERNELS[i][0].index(lo), lo, hi - lo + 1) for lo, hi in kept) for i, kept in enumerate(KEPT)
        )
        in_specs += [smem] + [vmem] * len(earlier)
        args += [log_scale.reshape(1), *earlier]
        scratch.append(pltpu.VMEM((16, lanes), jnp.float32))
    return pl.pallas_call(
        functools.partial(kernel, reads, sources, joins, height, width),
        out_shape=jax.ShapeDtypeStruct((16, 32 * LANES if earlier else lanes), jnp.float32),
        in_specs=in_specs,
        out_specs=vmem,
        scratch_shapes=scratch,
    )(*args)


def blocks_of(x, ids):
    runs, start = [], 0
    for i in range(1, len(ids) + 1):
        if i == len(ids) or ids[i] != ids[i - 1] + 1:
            runs.append(x[..., ids[start] * LANES : (ids[i - 1] + 1) * LANES])
            start = i
    return runs[0] if len(runs) == 1 else jnp.concatenate(runs, axis=-1)


def on_device(counts, weights):
    n_rows, n_cols = lax.axis_size("rows"), lax.axis_size("maps")
    height, width = n_rows * counts.shape[1], n_cols * counts.shape[2]
    r, m = lax.axis_index("rows"), lax.axis_index("maps")
    core = r % 2
    outer = ((r == 0) | (r == n_rows - 1)).astype(jnp.int32)
    scal = jnp.stack([core, outer, r * counts.shape[1], m * counts.shape[2]]).astype(jnp.int32)
    mix = weights / jnp.sum(weights)

    swap = [(i, i ^ 1) for i in range(n_rows)]
    hop = [(i, i + 2) for i in range(0, n_rows - 2, 2)] + [(i, i - 2) for i in range(3, n_rows, 2)]
    to_right = [(i, i + 1) for i in range(n_cols - 1)]
    to_left = [(i + 1, i) for i in range(n_cols - 1)]

    def after(x, *deps):
        return lax.optimization_barrier((x,) + deps)[0]

    def to_float(x):
        return x.astype(jnp.float32) + 1.0

    zo_own = to_float(lax.dynamic_slice_in_dim(counts, (1 - core) * 8, 8, axis=1))
    zo = lax.ppermute(zo_own, "rows", hop)
    n = to_float(after(counts, zo_own))
    own = [blocks_of(n, ids) for ids in CHUNKS]
    q = [lax.ppermute(x, "rows", swap) for x in own]
    zq = [lax.ppermute(x, "rows", hop) for x in q]

    sums = jnp.sum(n, axis=(1, 2))
    step = 0
    for axis, size in (("rows", n_rows), ("maps", n_cols)):
        bit = 1
        while bit < size:
            sums = sums + lax.ppermute(sums, axis, [(i, i ^ bit) for i in range(size)])
            bit, step = bit * 2, step + 1
    log_scale = jnp.sum(mix * jnp.log(float(height * width) / sums))

    f = [lax.ppermute(x, "rows", swap) for x in zq]

    def column(b):
        i = CHUNKS[0].index(b)
        cols = slice(i * LANES, (i + 1) * LANES)
        return jnp.concatenate(
            [zo[..., b * LANES : (b + 1) * LANES]] + [x[0][..., cols] for x in (zq, own, q, f)], axis=1
        )

    left = lax.ppermute(column(31), "maps", to_right)
    right = lax.ppermute(column(0), "maps", to_left)

    outs = []
    for which in range(len(KERNELS)):
        arrays = [zo]
        for c in KERNELS[which][1]:
            arrays += [own[c], q[c], zq[c], f[c]]
        if EDGE in KERNELS[which][0]:
            arrays += [left, right]
        earlier = outs if which == len(KERNELS) - 1 else []
        outs.append(run_kernel(which, height, width, scal, mix, arrays, earlier, log_scale))
    return outs[-1]


def solution(mesh):
    return jax.shard_map(
        on_device, mesh=mesh, in_specs=(P(None, "rows", "maps"), P()), out_specs=P("rows", "maps"), check_vma=False
    )
```

```python
import functools

import jax
import jax.numpy as jnp
import numpy as np
from jax import lax
from jax.experimental import pallas as pl
from jax.experimental.pallas import tpu as pltpu
from jax.sharding import PartitionSpec as P


HALF = 8
K = 8
LANES = 128
EDGE = -1

FIRST, SECOND = 12, 23
CHUNKS = (
    (29, 30, 31) + tuple(range(FIRST)),
    tuple(range(FIRST, SECOND)),
    tuple(range(SECOND, 29)),
)
KERNELS = (
    (tuple(range(FIRST)), (0,)),
    ((29, 30, 31, EDGE, 0, 1), (0,)),
    (tuple(range(FIRST - 3, SECOND)), (0, 1)),
    (tuple(range(SECOND - 2, 31)), (0, 1, 2)),
)
KEPT = (
    ((1, FIRST - 2),),
    ((30, 31), (0, 0)),
    ((FIRST - 1, SECOND - 2),),
    ((SECOND - 1, 29),),
)


def taps():
    spread = 0.45 * HALF
    a = np.arange(-HALF, HALF + 1, dtype=np.float64)
    g = np.exp(-a * a / (2.0 * spread * spread))
    return g / g.sum()


def band(out_pos, in_pos):
    g = taps()
    d = np.asarray(in_pos)[None, :] - np.asarray(out_pos)[:, None]
    return np.where(np.abs(d) <= HALF, g[np.clip(d + HALF, 0, 2 * HALF)], 0.0)


def split_np(x):
    x = np.asarray(x, np.float32)
    hi = x.astype(jnp.bfloat16)
    lo = (x - hi.astype(np.float32)).astype(jnp.bfloat16)
    return hi, lo


def positions(core):
    own = np.arange(16)
    if core == 0:
        zo, zq, q, f = np.arange(-24, -16), np.arange(-16, 0), np.arange(16, 32), np.arange(32, 40)
        z8, q8 = np.arange(-8, 0), np.arange(16, 24)
    else:
        zo, zq, q, f = np.arange(32, 40), np.arange(16, 32), np.arange(-16, 0), np.arange(-24, -16)
        z8, q8 = np.arange(16, 24), np.arange(-8, 0)
    return np.concatenate([zo, zq, own, q, f]), np.concatenate([zq, own, q]), np.concatenate([z8, own, q8]), own


def matrices():
    out = []
    for s in range(3):
        both = [split_np(band(positions(c)[s + 1], positions(c)[s])) for c in (0, 1)]
        out.append(np.stack([np.concatenate([h, l, h], axis=1) for h, l in both]))
    near = split_np(band(np.arange(256), np.arange(256)).T)
    lane = np.arange(LANES)
    far = split_np(band(np.arange(256), np.where(lane < 64, 256 + lane, lane - LANES)).T)
    out.append(np.concatenate([near[0], near[0], near[1], far[0], far[0], far[1]], axis=0))
    return out


def split(x):
    hi = x.astype(jnp.bfloat16)
    lo = (x - hi.astype(jnp.float32)).astype(jnp.bfloat16)
    return hi, lo


def dot(a, b):
    return jnp.dot(a, b, preferred_element_type=jnp.float32)


def row_pass(g, x):
    hi, lo = split(x)
    return split(dot(g, jnp.concatenate([hi, hi, lo], axis=0)))


def window_sum(pos, size):
    g = taps()
    total = jnp.zeros(pos.shape, jnp.float32)
    for i, a in enumerate(range(-HALF, HALF + 1)):
        total = total + jnp.where((pos + a >= 0) & (pos + a < size), np.float32(g[i]), np.float32(0.0))
    return total


def copies(reads, foff, zo, parts, halo, n_ref):
    where = {b: (c, i) for c, ids in enumerate(CHUNKS) for i, b in enumerate(ids)}
    out = []
    for at in range(0, len(reads), 2):
        pair = reads[at : at + 2]
        joined = EDGE not in pair and pair[1] == pair[0] + 1 and where[pair[1]] == (where[pair[0]][0], where[pair[0]][1] + 1)
        tile = []
        for i, b in enumerate(pair[:1] if joined else pair):
            size = (2 if joined else 1) * LANES
            dst = pl.ds((at + i) * LANES, size)
            if b == EDGE:
                tile.append((halo[1], n_ref.at[:, :, dst]))
                continue
            c, place = where[b]
            own, q, zq, f = parts[c]
            src = pl.ds(place * LANES, size)
            tile += [
                (zo.at[:, :, pl.ds(b * LANES, size)], n_ref.at[:, pl.ds(0, 8), dst]),
                (zq.at[:, :, src], n_ref.at[:, pl.ds(8, 16), dst]),
                (own.at[:, :, src], n_ref.at[:, pl.ds(24, 16), dst]),
                (q.at[:, :, src], n_ref.at[:, pl.ds(40, 16), dst]),
                (f.at[:, pl.ds(foff, 8), src], n_ref.at[:, pl.ds(56, 8), dst]),
            ]
        out.append(tile)
    return out


def edge_kernel(places, scal, zo, own, q, zq, f, left, right, sems):
    foff = pl.multiple_of(scal[0] * 8, 8)
    moves = []
    for (b, place), out in zip(places, (left, right)):
        src = pl.ds(place * LANES, LANES)
        moves += [
            (zo.at[:, :, pl.ds(b * LANES, LANES)], out.at[:, pl.ds(0, 8), :]),
            (zq.at[:, :, src], out.at[:, pl.ds(8, 16), :]),
            (own.at[:, :, src], out.at[:, pl.ds(24, 16), :]),
            (q.at[:, :, src], out.at[:, pl.ds(40, 16), :]),
            (f.at[:, pl.ds(foff, 8), src], out.at[:, pl.ds(56, 8), :]),
        ]
    moves = [pltpu.make_async_copy(src, dst, sems.at[i]) for i, (src, dst) in enumerate(moves)]
    for move in moves:
        move.start()
    for move in moves:
        move.wait()


def edge_columns(scal, *arrays):
    smem = pl.BlockSpec(memory_space=pltpu.SMEM)
    anywhere = pl.BlockSpec(memory_space=pl.ANY)
    vmem = pl.BlockSpec(memory_space=pltpu.VMEM)
    shape = jax.ShapeDtypeStruct((K, 64, LANES), jnp.float32)
    places = tuple((b, CHUNKS[0].index(b)) for b in (31, 0))
    return pl.pallas_call(
        functools.partial(edge_kernel, places),
        out_shape=(shape, shape),
        in_specs=[smem] + [anywhere] * len(arrays),
        out_specs=(vmem, vmem),
        scratch_shapes=[pltpu.SemaphoreType.DMA((10,))],
        name="edge_columns",
    )(scal, *arrays)


def kernel(reads, sources, joins, height, width, scal, mix, relcol, *refs):
    n_in = 1 + 4 * len(sources) + (2 if EDGE in reads else 0)
    zo = refs[0]
    parts = {c: refs[1 + 4 * i : 5 + 4 * i] for i, c in enumerate(sources)}
    halo = refs[1 + 4 * len(sources) : n_in]
    g1, g2, g3, bm = refs[n_in : n_in + 4]
    n_in += 4
    if joins:
        log_scale, earlier = refs[n_in], refs[n_in + 1 : n_in + len(joins)]
        n_in += len(joins)
    out = refs[n_in]
    n_ref, rr, rc, cv, h1h, h1l, h2h, h2l, h3h, h3l, u_ref, w_ref, sems = refs[n_in + 1 :][:13]
    acc_ref = refs[-1] if joins else out
    blocks = len(reads)
    tiles = blocks // 2
    core, outer, row0, col0 = scal[0], scal[1], scal[2], scal[3]
    foff = pl.multiple_of(core * 8, 8)

    for i, moves in enumerate(copies(reads, foff, zo, parts, halo, n_ref)):
        for src, dst in moves:
            pltpu.make_async_copy(src, dst, sems.at[i]).start()

    i = lax.broadcasted_iota(jnp.int32, (64, 256), 0)
    flipped = jnp.where(i < 8, i + 32, jnp.where(i < 24, i + 8, jnp.where(i < 40, i - 24, jnp.where(i < 56, i - 56, i - 80))))
    row = row0 + jnp.where(core == 0, i - 24, flipped)
    total = window_sum(row, height)
    rr[...] = jnp.where(total > 0.0, 1.0 / jnp.where(total > 0.0, total, 1.0), 0.0)
    col = col0 + relcol[...]
    total = window_sum(col, width)
    rc[...] = jnp.where(total > 0.0, 1.0 / jnp.where(total > 0.0, total, 1.0), 0.0)
    cv[...] = jnp.where((col >= 0) & (col < width), 1.0, 0.0)

    for ref in (h1h, h1l, h2h, h2l, h3h, h3l):
        rows = ref.shape[0]
        ref[:, 0:LANES] = jnp.zeros((rows, LANES), jnp.bfloat16)
        ref[:, pl.ds((blocks + 1) * LANES, LANES)] = jnp.zeros((rows, LANES), jnp.bfloat16)

    def tile(j):
        return pl.ds(pl.multiple_of(j * 256, 256), 256)

    def at(j, shift, size):
        return pl.ds(pl.multiple_of(j * 256 + shift, LANES), size)

    def column_pass(high, low, j):
        rows = high.shape[0]
        first = lax.broadcasted_iota(jnp.int32, (rows, LANES), 1) < 64
        mh, ml = high[:, at(j, LANES, 256)], low[:, at(j, LANES, 256)]
        eh = jnp.where(first, high[:, at(j, 3 * LANES, LANES)], high[:, at(j, 0, LANES)])
        el = jnp.where(first, low[:, at(j, 3 * LANES, LANES)], low[:, at(j, 0, LANES)])
        return dot(jnp.concatenate([mh, ml, mh, eh, el, eh], axis=1), bm[...])

    def arrived(j):
        window = n_ref.at[:, :, tile(j)]
        pltpu.make_async_copy(window, window, sems.at[j]).wait()

    if halo:
        for j in range(tiles):
            arrived(j)
        dst = pl.ds(reads.index(EDGE) * LANES, LANES)
        lane = lax.broadcasted_iota(jnp.int32, (K, 8, LANES), 2)
        for r in range(0, 64, 8):
            n_ref[:, r : r + 8, dst] = jnp.where(lane < 64, n_ref[:, r : r + 8, dst], halo[0][:, r : r + 8, :])

    def first(j):
        scale = rr[...] * rc[0:1, tile(j)]
        for k in range(K):
            hh, hl = row_pass(g1[core], n_ref[k, :, tile(j)] * scale)
            h1h[48 * k : 48 * k + 48, at(j, LANES, 256)] = hh
            h1l[48 * k : 48 * k + 48, at(j, LANES, 256)] = hl

    @pl.loop(0, tiles)
    def _(j):
        if not halo:
            arrived(j)
        first(j)

    def step(j, p):
        acc = jnp.zeros((48, 256), jnp.float32)
        for k in range(K):
            acc = acc + mix[k] * jnp.log(u_ref[p, 48 * k : 48 * k + 48, :])
        valid = cv[0:1, tile(j)] > 0.0
        index = lax.broadcasted_iota(jnp.int32, (48, 256), 0)
        valid = valid & ((index >= 16) | (outer == 0))
        geo = jnp.exp(acc)
        for k in range(K):
            w = jnp.where(valid, geo / u_ref[p, 48 * k : 48 * k + 48, :], 0.0)
            w_ref[k, :, tile(j)] = w[16:32]
            hh, hl = row_pass(g2[core], w)
            h2h[32 * k : 32 * k + 32, at(j, LANES, 256)] = hh
            h2l[32 * k : 32 * k + 32, at(j, LANES, 256)] = hl

    def stage(j, count):
        for p in range(count):
            u_ref[p] = column_pass(h1h, h1l, j + p)
        for p in range(count):
            step(j + p, p)

    @pl.loop(0, tiles // 2)
    def _(j):
        stage(2 * j, 2)

    if tiles % 2:
        stage(tiles - 1, 1)

    zrow = pl.ds(pl.multiple_of(jnp.where(core == 0, 16, 8), 8), 8)
    qrow = pl.ds(pl.multiple_of(jnp.where(core == 0, 40, 48), 8), 8)

    def step(j, p):
        valid = cv[0:1, tile(j)] > 0.0
        for k in range(K):
            n = jnp.concatenate([n_ref[k, zrow, tile(j)], n_ref[k, 24:40, tile(j)], n_ref[k, qrow, tile(j)]], axis=0)
            d = jnp.where(valid, n / u_ref[p, 32 * k : 32 * k + 32, :], 0.0)
            hh, hl = row_pass(g3[core], d)
            h3h[16 * k : 16 * k + 16, at(j, LANES, 256)] = hh
            h3l[16 * k : 16 * k + 16, at(j, LANES, 256)] = hl

    def stage(j, count):
        for p in range(count):
            u_ref[p, 0 : 32 * K, :] = column_pass(h2h, h2l, j + p)
        for p in range(count):
            step(j + p, p)

    @pl.loop(0, tiles // 2)
    def _(j):
        stage(2 * j, 2)

    if tiles % 2:
        stage(tiles - 1, 1)

    def step(j, p):
        acc = jnp.zeros((16, 256), jnp.float32)
        for k in range(K):
            acc = acc + mix[k] * jnp.log(w_ref[k, :, tile(j)] * u_ref[p, 16 * k : 16 * k + 16, :])
        acc_ref[:, tile(j)] = acc

    def stage(j, count):
        for p in range(count):
            u_ref[p, 0 : 16 * K, :] = column_pass(h3h, h3l, j + p)
        for p in range(count):
            step(j + p, p)

    @pl.loop(0, tiles // 2)
    def _(j):
        stage(2 * j, 2)

    if tiles % 2:
        stage(tiles - 1, 1)


    for i, moved in enumerate(joins):
        ref = acc_ref if i == len(joins) - 1 else earlier[i]
        for src, dst, count in moved:
            piece = ref[:, src * LANES : (src + count) * LANES] + log_scale[0]
            out[:, dst * LANES : (dst + count) * LANES] = jnp.exp(piece)


def relative_columns(reads):
    lane = np.arange(LANES)
    cols = [np.where(lane < 64, 4096 + lane, lane - LANES) if b == EDGE else b * LANES + lane for b in reads]
    return np.tile(np.concatenate(cols).astype(np.int32)[None], (8, 1))


def run_kernel(which, height, width, scal, mix, arrays, earlier, log_scale):
    reads, sources = KERNELS[which]
    blocks = len(reads)
    lanes = blocks * LANES
    wide = (blocks + 2) * LANES
    consts = matrices()
    smem = pl.BlockSpec(memory_space=pltpu.SMEM)
    vmem = pl.BlockSpec(memory_space=pltpu.VMEM)
    anywhere = pl.BlockSpec(memory_space=pl.ANY)
    scratch = [
        pltpu.VMEM((K, 64, lanes), jnp.float32),
        pltpu.VMEM((64, 256), jnp.float32),
        pltpu.VMEM((8, lanes), jnp.float32),
        pltpu.VMEM((8, lanes), jnp.float32),
    ]
    for rows in (48, 32, 16):
        scratch += [pltpu.VMEM((rows * K, wide), jnp.bfloat16)] * 2
    scratch += [
        pltpu.VMEM((2, 48 * K, 256), jnp.float32),
        pltpu.VMEM((K, 16, lanes), jnp.float32),
        pltpu.SemaphoreType.DMA((blocks // 2,)),
    ]
    halo_specs = [vmem, anywhere] if EDGE in reads else []
    in_specs = [smem, smem, vmem] + [anywhere] * (len(arrays) - len(halo_specs)) + halo_specs + [vmem] * len(consts)
    args = [scal, mix, jnp.asarray(relative_columns(reads)), *arrays, *[jnp.asarray(c) for c in consts]]
    joins = ()
    if earlier:
        joins = tuple(
            tuple((KERNELS[i][0].index(lo), lo, hi - lo + 1) for lo, hi in kept) for i, kept in enumerate(KEPT)
        )
        in_specs += [smem] + [vmem] * len(earlier)
        args += [log_scale.reshape(1), *earlier]
        scratch.append(pltpu.VMEM((16, lanes), jnp.float32))
    return pl.pallas_call(
        functools.partial(kernel, reads, sources, joins, height, width),
        out_shape=jax.ShapeDtypeStruct((16, 32 * LANES if earlier else lanes), jnp.float32),
        in_specs=in_specs,
        out_specs=vmem,
        scratch_shapes=scratch,
    )(*args)


def blocks_of(x, ids):
    runs, start = [], 0
    for i in range(1, len(ids) + 1):
        if i == len(ids) or ids[i] != ids[i - 1] + 1:
            runs.append(x[..., ids[start] * LANES : (ids[i - 1] + 1) * LANES])
            start = i
    return runs[0] if len(runs) == 1 else jnp.concatenate(runs, axis=-1)


def on_device(counts, weights):
    n_rows, n_cols = lax.axis_size("rows"), lax.axis_size("maps")
    height, width = n_rows * counts.shape[1], n_cols * counts.shape[2]
    r, m = lax.axis_index("rows"), lax.axis_index("maps")
    core = r % 2
    outer = ((r == 0) | (r == n_rows - 1)).astype(jnp.int32)
    scal = jnp.stack([core, outer, r * counts.shape[1], m * counts.shape[2]]).astype(jnp.int32)
    mix = lax.optimization_barrier(weights / jnp.sum(weights))

    swap = [(i, i ^ 1) for i in range(n_rows)]
    hop = [(i, i + 2) for i in range(0, n_rows - 2, 2)] + [(i, i - 2) for i in range(3, n_rows, 2)]
    to_right = [(i, i + 1) for i in range(n_cols - 1)]
    to_left = [(i + 1, i) for i in range(n_cols - 1)]

    def after(x, *deps):
        return lax.optimization_barrier((x,) + deps)[0]

    def to_float(x):
        return x.astype(jnp.float32) + 1.0

    zo_own = to_float(lax.dynamic_slice_in_dim(counts, (1 - core) * 8, 8, axis=1))
    zo = lax.ppermute(zo_own, "rows", hop)
    n = to_float(after(counts, zo_own))
    own = [blocks_of(n, ids) for ids in CHUNKS]
    q = [lax.ppermute(x, "rows", swap) for x in own]
    zq = [lax.ppermute(x, "rows", hop) for x in q]

    sums = jnp.sum(n, axis=(1, 2))
    rounds = [("rows", 1), ("maps", 1), ("maps", 2), ("rows", 16), ("rows", 32), ("rows", 2), ("rows", 4), ("rows", 8), ("maps", 4)]
    for axis, bit in rounds:
        sums = sums + lax.ppermute(sums, axis, [(d, d ^ bit) for d in range(lax.axis_size(axis))])
    log_scale = jnp.sum(mix * jnp.log(float(height * width) / sums))

    f = [lax.ppermute(x, "rows", swap) for x in zq]

    last, first = edge_columns(scal, zo, own[0], q[0], zq[0], f[0])
    left = lax.ppermute(last, "maps", to_right)
    right = lax.ppermute(first, "maps", to_left)

    outs = []
    for which in range(len(KERNELS)):
        arrays = [zo]
        for c in KERNELS[which][1]:
            arrays += [own[c], q[c], zq[c], f[c]]
        if EDGE in KERNELS[which][0]:
            arrays += [left, right]
        earlier = outs if which == len(KERNELS) - 1 else []
        outs.append(run_kernel(which, height, width, scal, mix, arrays, earlier, log_scale))
    return outs[-1]


def solution(mesh):
    return jax.shard_map(
        on_device, mesh=mesh, in_specs=(P(None, "rows", "maps"), P()), out_specs=P("rows", "maps"), check_vma=False
    )
```

```python
import functools

import jax
import jax.numpy as jnp
import numpy as np
from jax import lax
from jax.experimental import pallas as pl
from jax.experimental.pallas import tpu as pltpu
from jax.sharding import PartitionSpec as P


HALF = 8
K = 8
LANES = 128
EDGE = -1

FIRST = 22
CHUNKS = (tuple(range(FIRST)), tuple(range(FIRST, 32)) + (EDGE,))
KERNELS = (
    (tuple(range(FIRST)), (0,)),
    (tuple(range(FIRST - 3, 32)) + (EDGE, 0, 1), (0, 1)),
)
KEPT = (((1, FIRST - 2),), ((FIRST - 1, 31), (0, 0)))


def taps():
    spread = 0.45 * HALF
    a = np.arange(-HALF, HALF + 1, dtype=np.float64)
    g = np.exp(-a * a / (2.0 * spread * spread))
    return g / g.sum()


def band(out_pos, in_pos):
    g = taps()
    d = np.asarray(in_pos)[None, :] - np.asarray(out_pos)[:, None]
    return np.where(np.abs(d) <= HALF, g[np.clip(d + HALF, 0, 2 * HALF)], 0.0)


def split_np(x):
    x = np.asarray(x, np.float32)
    hi = x.astype(jnp.bfloat16)
    lo = (x - hi.astype(np.float32)).astype(jnp.bfloat16)
    return hi, lo


def positions(core):
    own = np.arange(16)
    if core == 0:
        zo, zq, q, f = np.arange(-24, -16), np.arange(-16, 0), np.arange(16, 32), np.arange(32, 40)
        z8, q8 = np.arange(-8, 0), np.arange(16, 24)
    else:
        zo, zq, q, f = np.arange(32, 40), np.arange(16, 32), np.arange(-16, 0), np.arange(-24, -16)
        z8, q8 = np.arange(16, 24), np.arange(-8, 0)
    return np.concatenate([zo, zq, own, q, f]), np.concatenate([zq, own, q]), np.concatenate([z8, own, q8]), own


def matrices():
    out = []
    for s in range(3):
        both = [split_np(band(positions(c)[s + 1], positions(c)[s])) for c in (0, 1)]
        out.append(np.stack([np.concatenate([h, l, h], axis=1) for h, l in both]))
    near = split_np(band(np.arange(256), np.arange(256)).T)
    lane = np.arange(LANES)
    far = split_np(band(np.arange(256), np.where(lane < 64, 256 + lane, lane - LANES)).T)
    out.append(np.concatenate([near[0], near[0], near[1], far[0], far[0], far[1]], axis=0))
    return out


def split(x):
    hi = x.astype(jnp.bfloat16)
    lo = (x - hi.astype(jnp.float32)).astype(jnp.bfloat16)
    return hi, lo


def dot(a, b):
    return jnp.dot(a, b, preferred_element_type=jnp.float32)


def row_pass(g, x):
    hi, lo = split(x)
    return split(dot(g, jnp.concatenate([hi, hi, lo], axis=0)))


def window_sum(pos, size):
    g = taps()
    total = jnp.zeros(pos.shape, jnp.float32)
    for i, a in enumerate(range(-HALF, HALF + 1)):
        total = total + jnp.where((pos + a >= 0) & (pos + a < size), np.float32(g[i]), np.float32(0.0))
    return total


def copies(reads, foff, parts, n_ref):
    where = {b: (c, i) for c, ids in enumerate(CHUNKS) for i, b in enumerate(ids)}
    out = []
    for at in range(0, len(reads), 2):
        (c, i), (d, j) = [where[b] for b in reads[at : at + 2]]
        tile = []
        for c, i, blocks, to in ((c, i, 2, at),) if (d, j) == (c, i + 1) else ((c, i, 1, at), (d, j, 1, at + 1)):
            zo, own, q, zq, f = parts[c]
            dst = pl.ds(to * LANES, blocks * LANES)
            src = pl.ds(i * LANES, blocks * LANES)
            tile += [
                (zo.at[:, :, src], n_ref.at[:, pl.ds(0, 8), dst]),
                (zq.at[:, :, src], n_ref.at[:, pl.ds(8, 16), dst]),
                (own.at[:, :, src], n_ref.at[:, pl.ds(24, 16), dst]),
                (q.at[:, :, src], n_ref.at[:, pl.ds(40, 16), dst]),
                (f.at[:, pl.ds(foff, 8), src], n_ref.at[:, pl.ds(56, 8), dst]),
            ]
        out.append(tile)
    return out


def kernel(reads, sources, joins, height, width, scal, mix, relcol, *refs):
    n_in = 5 * len(sources)
    parts = {c: refs[5 * i : 5 * i + 5] for i, c in enumerate(sources)}
    g1, g2, g3, bm = refs[n_in : n_in + 4]
    n_in += 4
    if joins:
        log_scale, earlier = refs[n_in], refs[n_in + 1 : n_in + len(joins)]
        n_in += len(joins)
    out = refs[n_in]
    n_ref, rr, rc, cv, h1h, h1l, h2h, h2l, h3h, h3l, u_ref, w_ref, sems = refs[n_in + 1 :][:13]
    acc_ref = refs[-1] if joins else out
    blocks = len(reads)
    tiles = blocks // 2
    core, outer, row0, col0 = scal[0], scal[1], scal[2], scal[3]
    foff = pl.multiple_of(core * 8, 8)

    for i, moves in enumerate(copies(reads, foff, parts, n_ref)):
        for src, dst in moves:
            pltpu.make_async_copy(src, dst, sems.at[i]).start()

    i = lax.broadcasted_iota(jnp.int32, (64, 256), 0)
    flipped = jnp.where(i < 8, i + 32, jnp.where(i < 24, i + 8, jnp.where(i < 40, i - 24, jnp.where(i < 56, i - 56, i - 80))))
    row = row0 + jnp.where(core == 0, i - 24, flipped)
    total = window_sum(row, height)
    rr[...] = jnp.where(total > 0.0, 1.0 / jnp.where(total > 0.0, total, 1.0), 0.0)
    col = col0 + relcol[...]
    total = window_sum(col, width)
    rc[...] = jnp.where(total > 0.0, 1.0 / jnp.where(total > 0.0, total, 1.0), 0.0)
    cv[...] = jnp.where((col >= 0) & (col < width), 1.0, 0.0)

    for ref in (h1h, h1l, h2h, h2l, h3h, h3l):
        rows = ref.shape[0]
        ref[:, 0:LANES] = jnp.zeros((rows, LANES), jnp.bfloat16)
        ref[:, pl.ds((blocks + 1) * LANES, LANES)] = jnp.zeros((rows, LANES), jnp.bfloat16)

    def tile(j):
        return pl.ds(pl.multiple_of(j * 256, 256), 256)

    def at(j, shift, size):
        return pl.ds(pl.multiple_of(j * 256 + shift, LANES), size)

    def column_pass(high, low, j):
        rows = high.shape[0]
        first = lax.broadcasted_iota(jnp.int32, (rows, LANES), 1) < 64
        mh, ml = high[:, at(j, LANES, 256)], low[:, at(j, LANES, 256)]
        eh = jnp.where(first, high[:, at(j, 3 * LANES, LANES)], high[:, at(j, 0, LANES)])
        el = jnp.where(first, low[:, at(j, 3 * LANES, LANES)], low[:, at(j, 0, LANES)])
        return dot(jnp.concatenate([mh, ml, mh, eh, el, eh], axis=1), bm[...])

    def arrived(j):
        window = n_ref.at[:, :, tile(j)]
        pltpu.make_async_copy(window, window, sems.at[j]).wait()

    def first(j):
        scale = rr[...] * rc[0:1, tile(j)]
        for k in range(K):
            hh, hl = row_pass(g1[core], n_ref[k, :, tile(j)] * scale)
            h1h[48 * k : 48 * k + 48, at(j, LANES, 256)] = hh
            h1l[48 * k : 48 * k + 48, at(j, LANES, 256)] = hl

    def stage(j, count):
        for p in range(count):
            arrived(j + p)
        for p in range(count):
            first(j + p)

    @pl.loop(0, tiles // 2)
    def _(j):
        stage(2 * j, 2)

    if tiles % 2:
        stage(tiles - 1, 1)

    def step(j, p):
        acc = jnp.zeros((48, 256), jnp.float32)
        for k in range(K):
            acc = acc + mix[k] * jnp.log(u_ref[p, 48 * k : 48 * k + 48, :])
        valid = cv[0:1, tile(j)] > 0.0
        index = lax.broadcasted_iota(jnp.int32, (48, 256), 0)
        valid = valid & ((index >= 16) | (outer == 0))
        geo = jnp.exp(acc)
        for k in range(K):
            w = jnp.where(valid, geo / u_ref[p, 48 * k : 48 * k + 48, :], 0.0)
            w_ref[k, :, tile(j)] = w[16:32]
            hh, hl = row_pass(g2[core], w)
            h2h[32 * k : 32 * k + 32, at(j, LANES, 256)] = hh
            h2l[32 * k : 32 * k + 32, at(j, LANES, 256)] = hl

    def stage(j, count):
        for p in range(count):
            u_ref[p] = column_pass(h1h, h1l, j + p)
        for p in range(count):
            step(j + p, p)

    @pl.loop(0, tiles // 2)
    def _(j):
        stage(2 * j, 2)

    if tiles % 2:
        stage(tiles - 1, 1)

    zrow = pl.ds(pl.multiple_of(jnp.where(core == 0, 16, 8), 8), 8)
    qrow = pl.ds(pl.multiple_of(jnp.where(core == 0, 40, 48), 8), 8)

    def step(j, p):
        valid = cv[0:1, tile(j)] > 0.0
        for k in range(K):
            n = jnp.concatenate([n_ref[k, zrow, tile(j)], n_ref[k, 24:40, tile(j)], n_ref[k, qrow, tile(j)]], axis=0)
            d = jnp.where(valid, n / u_ref[p, 32 * k : 32 * k + 32, :], 0.0)
            hh, hl = row_pass(g3[core], d)
            h3h[16 * k : 16 * k + 16, at(j, LANES, 256)] = hh
            h3l[16 * k : 16 * k + 16, at(j, LANES, 256)] = hl

    def stage(j, count):
        for p in range(count):
            u_ref[p, 0 : 32 * K, :] = column_pass(h2h, h2l, j + p)
        for p in range(count):
            step(j + p, p)

    @pl.loop(0, tiles // 2)
    def _(j):
        stage(2 * j, 2)

    if tiles % 2:
        stage(tiles - 1, 1)

    def step(j, p):
        acc = jnp.zeros((16, 256), jnp.float32)
        for k in range(K):
            acc = acc + mix[k] * jnp.log(w_ref[k, :, tile(j)] * u_ref[p, 16 * k : 16 * k + 16, :])
        acc_ref[:, tile(j)] = acc

    def stage(j, count):
        for p in range(count):
            u_ref[p, 0 : 16 * K, :] = column_pass(h3h, h3l, j + p)
        for p in range(count):
            step(j + p, p)

    @pl.loop(0, tiles // 2)
    def _(j):
        stage(2 * j, 2)

    if tiles % 2:
        stage(tiles - 1, 1)


    for i, moved in enumerate(joins):
        ref = acc_ref if i == len(joins) - 1 else earlier[i]
        for src, dst, count in moved:
            piece = ref[:, src * LANES : (src + count) * LANES] + log_scale[0]
            out[:, dst * LANES : (dst + count) * LANES] = jnp.exp(piece)


def relative_columns(reads):
    lane = np.arange(LANES)
    cols = [np.where(lane < 64, 4096 + lane, lane - LANES) if b == EDGE else b * LANES + lane for b in reads]
    return np.tile(np.concatenate(cols).astype(np.int32)[None], (8, 1))


def run_kernel(which, height, width, scal, mix, arrays, earlier, log_scale):
    reads, sources = KERNELS[which]
    blocks = len(reads)
    lanes = blocks * LANES
    wide = (blocks + 2) * LANES
    consts = matrices()
    smem = pl.BlockSpec(memory_space=pltpu.SMEM)
    vmem = pl.BlockSpec(memory_space=pltpu.VMEM)
    anywhere = pl.BlockSpec(memory_space=pl.ANY)
    scratch = [
        pltpu.VMEM((K, 64, lanes), jnp.float32),
        pltpu.VMEM((64, 256), jnp.float32),
        pltpu.VMEM((8, lanes), jnp.float32),
        pltpu.VMEM((8, lanes), jnp.float32),
    ]
    for rows in (48, 32, 16):
        scratch += [pltpu.VMEM((rows * K, wide), jnp.bfloat16)] * 2
    scratch += [
        pltpu.VMEM((2, 48 * K, 256), jnp.float32),
        pltpu.VMEM((K, 16, lanes), jnp.float32),
        pltpu.SemaphoreType.DMA((blocks // 2,)),
    ]
    in_specs = [smem, smem, vmem] + [anywhere] * len(arrays) + [vmem] * len(consts)
    args = [scal, mix, jnp.asarray(relative_columns(reads)), *arrays, *[jnp.asarray(c) for c in consts]]
    joins = ()
    if earlier:
        joins = tuple(
            tuple((KERNELS[i][0].index(lo), lo, hi - lo + 1) for lo, hi in kept) for i, kept in enumerate(KEPT)
        )
        in_specs += [smem] + [vmem] * len(earlier)
        args += [log_scale.reshape(1), *earlier]
        scratch.append(pltpu.VMEM((16, lanes), jnp.float32))
    return pl.pallas_call(
        functools.partial(kernel, reads, sources, joins, height, width),
        out_shape=jax.ShapeDtypeStruct((16, 32 * LANES if earlier else lanes), jnp.float32),
        in_specs=in_specs,
        out_specs=vmem,
        scratch_shapes=scratch,
    )(*args)


def on_device(counts, weights):
    n_rows, n_cols = lax.axis_size("rows"), lax.axis_size("maps")
    height, width = n_rows * counts.shape[1], n_cols * counts.shape[2]
    r, m = lax.axis_index("rows"), lax.axis_index("maps")
    core = r % 2
    outer = ((r == 0) | (r == n_rows - 1)).astype(jnp.int32)
    scal = jnp.stack([core, outer, r * counts.shape[1], m * counts.shape[2]]).astype(jnp.int32)
    mix = lax.optimization_barrier(weights / jnp.sum(weights))

    swap = [(i, i ^ 1) for i in range(n_rows)]
    hop = [(i, i + 2) for i in range(0, n_rows - 2, 2)] + [(i, i - 2) for i in range(3, n_rows, 2)]
    to_right = [(i, i + 1) for i in range(n_cols - 1)]
    to_left = [(i + 1, i) for i in range(n_cols - 1)]

    def after(x, *deps):
        return lax.optimization_barrier((x,) + deps)[0]

    def to_float(x):
        return x.astype(jnp.float32) + 1.0

    def outward(x):
        return lax.dynamic_slice_in_dim(x, (1 - core) * 8, 8, axis=1)

    edge = FIRST * LANES
    zo_own = to_float(outward(counts[..., :edge]))
    zo = [lax.ppermute(zo_own, "rows", hop)]
    n = to_float(after(counts, zo_own))
    left = lax.ppermute(n[..., -LANES:], "maps", to_right)
    right = lax.ppermute(n[..., :LANES], "maps", to_left)
    lane = lax.broadcasted_iota(jnp.int32, left.shape, 2)
    own = [n[..., :edge], jnp.concatenate([n[..., edge:], jnp.where(lane < 64, right, left)], axis=-1)]
    zo.append(lax.ppermute(outward(own[1]), "rows", hop))
    q = [lax.ppermute(x, "rows", swap) for x in own]
    zq = [lax.ppermute(x, "rows", hop) for x in q]
    f = [lax.ppermute(x, "rows", swap) for x in zq]

    sums = jnp.sum(n, axis=(1, 2))
    rounds = [("maps", 4), ("rows", 1), ("maps", 1), ("maps", 2), ("rows", 16), ("rows", 32), ("rows", 2), ("rows", 4), ("rows", 8)]
    for axis, bit in rounds:
        sums = sums + lax.ppermute(sums, axis, [(d, d ^ bit) for d in range(lax.axis_size(axis))])
    log_scale = jnp.sum(mix * jnp.log(float(height * width) / sums))

    outs = []
    for which in range(len(KERNELS)):
        arrays = []
        for c in KERNELS[which][1]:
            arrays += [zo[c], own[c], q[c], zq[c], f[c]]
        earlier = outs if which == len(KERNELS) - 1 else []
        outs.append(run_kernel(which, height, width, scal, mix, arrays, earlier, log_scale))
    return outs[-1]


def solution(mesh):
    return jax.shard_map(
        on_device, mesh=mesh, in_specs=(P(None, "rows", "maps"), P()), out_specs=P("rows", "maps"), check_vma=False
    )
```

```python
import functools

import jax
import jax.numpy as jnp
import numpy as np
from jax import lax
from jax.experimental import pallas as pl
from jax.experimental.pallas import tpu as pltpu
from jax.sharding import PartitionSpec as P


HALF = 8
K = 8
LANES = 128
EDGE = -1

FIRST = 22
CHUNKS = (tuple(range(FIRST)), tuple(range(FIRST, 32)) + (EDGE,))
KERNELS = (
    (tuple(range(FIRST)), (0,)),
    (tuple(range(FIRST - 3, 32)) + (EDGE, 0, 1), (0, 1)),
)
KEPT = (((1, FIRST - 2),), ((FIRST - 1, 31), (0, 0)))


def taps():
    spread = 0.45 * HALF
    a = np.arange(-HALF, HALF + 1, dtype=np.float64)
    g = np.exp(-a * a / (2.0 * spread * spread))
    return g / g.sum()


def band(out_pos, in_pos):
    g = taps()
    d = np.asarray(in_pos)[None, :] - np.asarray(out_pos)[:, None]
    return np.where(np.abs(d) <= HALF, g[np.clip(d + HALF, 0, 2 * HALF)], 0.0)


def split_np(x):
    x = np.asarray(x, np.float32)
    hi = x.astype(jnp.bfloat16)
    lo = (x - hi.astype(np.float32)).astype(jnp.bfloat16)
    return hi, lo


def positions(core):
    own = np.arange(16)
    if core == 0:
        zo, zq, q, f = np.arange(-24, -16), np.arange(-16, 0), np.arange(16, 32), np.arange(32, 40)
        z8, q8 = np.arange(-8, 0), np.arange(16, 24)
    else:
        zo, zq, q, f = np.arange(32, 40), np.arange(16, 32), np.arange(-16, 0), np.arange(-24, -16)
        z8, q8 = np.arange(16, 24), np.arange(-8, 0)
    return np.concatenate([zo, zq, own, q, f]), np.concatenate([zq, own, q]), np.concatenate([z8, own, q8]), own


def matrices():
    out = []
    for s in range(3):
        both = [split_np(band(positions(c)[s + 1], positions(c)[s])) for c in (0, 1)]
        out.append(np.stack([np.concatenate([h, l, h], axis=1) for h, l in both]))
    near = split_np(band(np.arange(256), np.arange(256)).T)
    lane = np.arange(LANES)
    far = split_np(band(np.arange(256), np.where(lane < 64, 256 + lane, lane - LANES)).T)
    out.append(np.concatenate([near[0], near[0], near[1], far[0], far[0], far[1]], axis=0))
    return out


def split(x):
    hi = x.astype(jnp.bfloat16)
    lo = (x - hi.astype(jnp.float32)).astype(jnp.bfloat16)
    return hi, lo


def dot(a, b):
    return jnp.dot(a, b, preferred_element_type=jnp.float32)


def row_pass(g, x):
    hi, lo = split(x)
    return split(dot(g, jnp.concatenate([hi, hi, lo], axis=0)))


def window_sum(pos, size):
    g = taps()
    total = jnp.zeros(pos.shape, jnp.float32)
    for i, a in enumerate(range(-HALF, HALF + 1)):
        total = total + jnp.where((pos + a >= 0) & (pos + a < size), np.float32(g[i]), np.float32(0.0))
    return total


def copies(reads, foff, parts, n_ref):
    where = {b: (c, i) for c, ids in enumerate(CHUNKS) for i, b in enumerate(ids)}
    out = []
    for at in range(0, len(reads), 2):
        (c, i), (d, j) = [where[b] for b in reads[at : at + 2]]
        tile = []
        for c, i, blocks, to in ((c, i, 2, at),) if (d, j) == (c, i + 1) else ((c, i, 1, at), (d, j, 1, at + 1)):
            zo, own, q, zq, f = parts[c]
            dst = pl.ds(to * LANES, blocks * LANES)
            src = pl.ds(i * LANES, blocks * LANES)
            tile += [
                (zo.at[:, :, src], n_ref.at[:, pl.ds(0, 8), dst]),
                (zq.at[:, :, src], n_ref.at[:, pl.ds(8, 16), dst]),
                (own.at[:, :, src], n_ref.at[:, pl.ds(24, 16), dst]),
                (q.at[:, :, src], n_ref.at[:, pl.ds(40, 16), dst]),
                (f.at[:, pl.ds(foff, 8), src], n_ref.at[:, pl.ds(56, 8), dst]),
            ]
        out.append(tile)
    return out


def kernel(reads, sources, joins, height, width, scal, mix, relcol, *refs):
    n_in = 5 * len(sources)
    parts = {c: refs[5 * i : 5 * i + 5] for i, c in enumerate(sources)}
    g1, g2, g3, bm = refs[n_in : n_in + 4]
    n_in += 4
    if joins:
        earlier = refs[n_in : n_in + len(joins) - 1]
        n_in += len(joins) - 1
    out = refs[n_in]
    n_ref, rr, rc, cv, h1h, h1l, h2h, h2l, h3h, h3l, u_ref, w_ref, sems = refs[n_in + 1 :][:13]
    acc_ref = refs[-1] if joins else out
    blocks = len(reads)
    tiles = blocks // 2
    core, outer, row0, col0 = scal[0], scal[1], scal[2], scal[3]
    foff = pl.multiple_of(core * 8, 8)

    for i, moves in enumerate(copies(reads, foff, parts, n_ref)):
        for src, dst in moves:
            pltpu.make_async_copy(src, dst, sems.at[i]).start()

    i = lax.broadcasted_iota(jnp.int32, (64, 256), 0)
    flipped = jnp.where(i < 8, i + 32, jnp.where(i < 24, i + 8, jnp.where(i < 40, i - 24, jnp.where(i < 56, i - 56, i - 80))))
    row = row0 + jnp.where(core == 0, i - 24, flipped)
    total = window_sum(row, height)
    rr[...] = jnp.where(total > 0.0, 1.0 / jnp.where(total > 0.0, total, 1.0), 0.0)
    col = col0 + relcol[...]
    total = window_sum(col, width)
    rc[...] = jnp.where(total > 0.0, 1.0 / jnp.where(total > 0.0, total, 1.0), 0.0)
    cv[...] = jnp.where((col >= 0) & (col < width), 1.0, 0.0)

    for ref in (h1h, h1l, h2h, h2l, h3h, h3l):
        rows = ref.shape[0]
        ref[:, 0:LANES] = jnp.zeros((rows, LANES), jnp.bfloat16)
        ref[:, pl.ds((blocks + 1) * LANES, LANES)] = jnp.zeros((rows, LANES), jnp.bfloat16)

    def tile(j):
        return pl.ds(pl.multiple_of(j * 256, 256), 256)

    def at(j, shift, size):
        return pl.ds(pl.multiple_of(j * 256 + shift, LANES), size)

    def column_pass(high, low, j):
        rows = high.shape[0]
        first = lax.broadcasted_iota(jnp.int32, (rows, LANES), 1) < 64
        mh, ml = high[:, at(j, LANES, 256)], low[:, at(j, LANES, 256)]
        eh = jnp.where(first, high[:, at(j, 3 * LANES, LANES)], high[:, at(j, 0, LANES)])
        el = jnp.where(first, low[:, at(j, 3 * LANES, LANES)], low[:, at(j, 0, LANES)])
        return dot(jnp.concatenate([mh, ml, mh, eh, el, eh], axis=1), bm[...])

    def arrived(j):
        window = n_ref.at[:, :, tile(j)]
        pltpu.make_async_copy(window, window, sems.at[j]).wait()

    def first(j):
        scale = rr[...] * rc[0:1, tile(j)]
        for k in range(K):
            hh, hl = row_pass(g1[core], n_ref[k, :, tile(j)] * scale)
            h1h[48 * k : 48 * k + 48, at(j, LANES, 256)] = hh
            h1l[48 * k : 48 * k + 48, at(j, LANES, 256)] = hl

    def stage(j, count):
        for p in range(count):
            arrived(j + p)
        for p in range(count):
            first(j + p)

    @pl.loop(0, tiles // 2)
    def _(j):
        stage(2 * j, 2)

    if tiles % 2:
        stage(tiles - 1, 1)

    def step(j, p):
        acc = jnp.zeros((48, 256), jnp.float32)
        for k in range(K):
            acc = acc + mix[k] * jnp.log(u_ref[p, 48 * k : 48 * k + 48, :])
        valid = cv[0:1, tile(j)] > 0.0
        index = lax.broadcasted_iota(jnp.int32, (48, 256), 0)
        valid = valid & ((index >= 16) | (outer == 0))
        geo = jnp.exp(acc)
        for k in range(K):
            w = jnp.where(valid, geo / u_ref[p, 48 * k : 48 * k + 48, :], 0.0)
            w_ref[k, :, tile(j)] = w[16:32]
            hh, hl = row_pass(g2[core], w)
            h2h[32 * k : 32 * k + 32, at(j, LANES, 256)] = hh
            h2l[32 * k : 32 * k + 32, at(j, LANES, 256)] = hl

    def stage(j, count):
        for p in range(count):
            u_ref[p] = column_pass(h1h, h1l, j + p)
        for p in range(count):
            step(j + p, p)

    @pl.loop(0, tiles // 2)
    def _(j):
        stage(2 * j, 2)

    if tiles % 2:
        stage(tiles - 1, 1)

    zrow = pl.ds(pl.multiple_of(jnp.where(core == 0, 16, 8), 8), 8)
    qrow = pl.ds(pl.multiple_of(jnp.where(core == 0, 40, 48), 8), 8)

    def step(j, p):
        valid = cv[0:1, tile(j)] > 0.0
        for k in range(K):
            n = jnp.concatenate([n_ref[k, zrow, tile(j)], n_ref[k, 24:40, tile(j)], n_ref[k, qrow, tile(j)]], axis=0)
            d = jnp.where(valid, n / u_ref[p, 32 * k : 32 * k + 32, :], 0.0)
            hh, hl = row_pass(g3[core], d)
            h3h[16 * k : 16 * k + 16, at(j, LANES, 256)] = hh
            h3l[16 * k : 16 * k + 16, at(j, LANES, 256)] = hl

    def stage(j, count):
        for p in range(count):
            u_ref[p, 0 : 32 * K, :] = column_pass(h2h, h2l, j + p)
        for p in range(count):
            step(j + p, p)

    @pl.loop(0, tiles // 2)
    def _(j):
        stage(2 * j, 2)

    if tiles % 2:
        stage(tiles - 1, 1)

    def step(j, p):
        acc = jnp.zeros((16, 256), jnp.float32)
        for k in range(K):
            acc = acc + mix[k] * jnp.log(w_ref[k, :, tile(j)] * u_ref[p, 16 * k : 16 * k + 16, :])
        acc_ref[:, tile(j)] = acc

    def stage(j, count):
        for p in range(count):
            u_ref[p, 0 : 16 * K, :] = column_pass(h3h, h3l, j + p)
        for p in range(count):
            step(j + p, p)

    @pl.loop(0, tiles // 2)
    def _(j):
        stage(2 * j, 2)

    if tiles % 2:
        stage(tiles - 1, 1)


    for i, moved in enumerate(joins):
        ref = acc_ref if i == len(joins) - 1 else earlier[i]
        for src, dst, count in moved:
            out[:, dst * LANES : (dst + count) * LANES] = ref[:, src * LANES : (src + count) * LANES]


def relative_columns(reads):
    lane = np.arange(LANES)
    cols = [np.where(lane < 64, 4096 + lane, lane - LANES) if b == EDGE else b * LANES + lane for b in reads]
    return np.tile(np.concatenate(cols).astype(np.int32)[None], (8, 1))


def run_kernel(which, height, width, scal, mix, arrays, earlier):
    reads, sources = KERNELS[which]
    blocks = len(reads)
    lanes = blocks * LANES
    wide = (blocks + 2) * LANES
    consts = matrices()
    smem = pl.BlockSpec(memory_space=pltpu.SMEM)
    vmem = pl.BlockSpec(memory_space=pltpu.VMEM)
    anywhere = pl.BlockSpec(memory_space=pl.ANY)
    scratch = [
        pltpu.VMEM((K, 64, lanes), jnp.float32),
        pltpu.VMEM((64, 256), jnp.float32),
        pltpu.VMEM((8, lanes), jnp.float32),
        pltpu.VMEM((8, lanes), jnp.float32),
    ]
    for rows in (48, 32, 16):
        scratch += [pltpu.VMEM((rows * K, wide), jnp.bfloat16)] * 2
    scratch += [
        pltpu.VMEM((2, 48 * K, 256), jnp.float32),
        pltpu.VMEM((K, 16, lanes), jnp.float32),
        pltpu.SemaphoreType.DMA((blocks // 2,)),
    ]
    in_specs = [smem, smem, vmem] + [anywhere] * len(arrays) + [vmem] * len(consts)
    args = [scal, mix, jnp.asarray(relative_columns(reads)), *arrays, *[jnp.asarray(c) for c in consts]]
    joins = ()
    if earlier:
        joins = tuple(
            tuple((KERNELS[i][0].index(lo), lo, hi - lo + 1) for lo, hi in kept) for i, kept in enumerate(KEPT)
        )
        in_specs += [vmem] * len(earlier)
        args += earlier
        scratch.append(pltpu.VMEM((16, lanes), jnp.float32))
    return pl.pallas_call(
        functools.partial(kernel, reads, sources, joins, height, width),
        out_shape=jax.ShapeDtypeStruct((16, 32 * LANES if earlier else lanes), jnp.float32),
        in_specs=in_specs,
        out_specs=vmem,
        scratch_shapes=scratch,
    )(*args)


def on_device(counts, weights):
    n_rows, n_cols = lax.axis_size("rows"), lax.axis_size("maps")
    height, width = n_rows * counts.shape[1], n_cols * counts.shape[2]
    r, m = lax.axis_index("rows"), lax.axis_index("maps")
    core = r % 2
    outer = ((r == 0) | (r == n_rows - 1)).astype(jnp.int32)
    scal = jnp.stack([core, outer, r * counts.shape[1], m * counts.shape[2]]).astype(jnp.int32)
    mix = lax.optimization_barrier(weights / jnp.sum(weights))

    swap = [(i, i ^ 1) for i in range(n_rows)]
    hop = [(i, i + 2) for i in range(0, n_rows - 2, 2)] + [(i, i - 2) for i in range(3, n_rows, 2)]
    to_right = [(i, i + 1) for i in range(n_cols - 1)]
    to_left = [(i + 1, i) for i in range(n_cols - 1)]

    def after(x, *deps):
        return lax.optimization_barrier((x,) + deps)[0]

    def to_float(x):
        return x.astype(jnp.float32) + 1.0

    def outward(x):
        return lax.dynamic_slice_in_dim(x, (1 - core) * 8, 8, axis=1)

    edge = FIRST * LANES
    zo_own = to_float(outward(counts[..., :edge]))
    zo = [lax.ppermute(zo_own, "rows", hop)]
    n = to_float(after(counts, zo_own))
    left = lax.ppermute(n[..., -LANES:], "maps", to_right)
    right = lax.ppermute(n[..., :LANES], "maps", to_left)
    lane = lax.broadcasted_iota(jnp.int32, left.shape, 2)
    own = [n[..., :edge], jnp.concatenate([n[..., edge:], jnp.where(lane < 64, right, left)], axis=-1)]
    zo.append(lax.ppermute(outward(own[1]), "rows", hop))
    q = [lax.ppermute(x, "rows", swap) for x in own]
    zq = [lax.ppermute(x, "rows", hop) for x in q]
    f = [lax.ppermute(x, "rows", swap) for x in zq]

    sums = jnp.sum(n, axis=(1, 2))
    rounds = [("maps", 4), ("rows", 1), ("maps", 1), ("maps", 2), ("rows", 16), ("rows", 32), ("rows", 2), ("rows", 4), ("rows", 8)]
    for axis, bit in rounds:
        sums = sums + lax.ppermute(sums, axis, [(d, d ^ bit) for d in range(lax.axis_size(axis))])
    log_scale = jnp.sum(mix * jnp.log(float(height * width) / sums))

    outs = []
    for which in range(len(KERNELS)):
        arrays = []
        for c in KERNELS[which][1]:
            arrays += [zo[c], own[c], q[c], zq[c], f[c]]
        earlier = outs if which == len(KERNELS) - 1 else []
        outs.append(run_kernel(which, height, width, scal, mix, arrays, earlier))
    return jnp.exp(outs[-1] + log_scale)


def solution(mesh):
    return jax.shard_map(
        on_device, mesh=mesh, in_specs=(P(None, "rows", "maps"), P()), out_specs=P("rows", "maps"), check_vma=False
    )
```

```python
import functools

import jax
import jax.numpy as jnp
import numpy as np
from jax import lax
from jax.experimental import pallas as pl
from jax.experimental.pallas import tpu as pltpu
from jax.sharding import PartitionSpec as P


HALF = 8
K = 8
LANES = 128
EDGE = -1

FIRST = 22
CHUNKS = (tuple(range(FIRST)), tuple(range(FIRST, 32)) + (EDGE,))
KERNELS = (
    (tuple(range(FIRST)), (0,)),
    (tuple(range(FIRST - 3, 32)) + (EDGE, 0, 1), (0, 1)),
)
KEPT = (((1, FIRST - 2),), ((FIRST - 1, 31), (0, 0)))


def taps():
    spread = 0.45 * HALF
    a = np.arange(-HALF, HALF + 1, dtype=np.float64)
    g = np.exp(-a * a / (2.0 * spread * spread))
    return g / g.sum()


def band(out_pos, in_pos):
    g = taps()
    d = np.asarray(in_pos)[None, :] - np.asarray(out_pos)[:, None]
    return np.where(np.abs(d) <= HALF, g[np.clip(d + HALF, 0, 2 * HALF)], 0.0)


def split_np(x):
    x = np.asarray(x, np.float32)
    hi = x.astype(jnp.bfloat16)
    lo = (x - hi.astype(np.float32)).astype(jnp.bfloat16)
    return hi, lo


def positions(core):
    own = np.arange(16)
    if core == 0:
        zo, zq, q, f = np.arange(-24, -16), np.arange(-16, 0), np.arange(16, 32), np.arange(32, 40)
        z8, q8 = np.arange(-8, 0), np.arange(16, 24)
    else:
        zo, zq, q, f = np.arange(32, 40), np.arange(16, 32), np.arange(-16, 0), np.arange(-24, -16)
        z8, q8 = np.arange(16, 24), np.arange(-8, 0)
    return np.concatenate([zo, zq, own, q, f]), np.concatenate([zq, own, q]), np.concatenate([z8, own, q8]), own


def matrices():
    out = []
    for s in range(3):
        both = [split_np(band(positions(c)[s + 1], positions(c)[s])) for c in (0, 1)]
        out.append(np.stack([np.concatenate([h, l, h], axis=1) for h, l in both]))
    near = split_np(band(np.arange(256), np.arange(256)).T)
    lane = np.arange(LANES)
    far = split_np(band(np.arange(256), np.where(lane < 64, 256 + lane, lane - LANES)).T)
    out.append(np.concatenate([near[0], near[0], near[1], far[0], far[0], far[1]], axis=0))
    return out


def split(x):
    hi = x.astype(jnp.bfloat16)
    lo = (x - hi.astype(jnp.float32)).astype(jnp.bfloat16)
    return hi, lo


def dot(a, b):
    return jnp.dot(a, b, preferred_element_type=jnp.float32)


def row_pass(g, x):
    hi, lo = split(x)
    return split(dot(g, jnp.concatenate([hi, hi, lo], axis=0)))


def window_sum(pos, size):
    g = taps()
    total = jnp.zeros(pos.shape, jnp.float32)
    for i, a in enumerate(range(-HALF, HALF + 1)):
        total = total + jnp.where((pos + a >= 0) & (pos + a < size), np.float32(g[i]), np.float32(0.0))
    return total


def copies(reads, foff, parts, n_ref):
    where = {b: (c, i) for c, ids in enumerate(CHUNKS) for i, b in enumerate(ids)}
    out = []
    for at in range(0, len(reads), 2):
        (c, i), (d, j) = [where[b] for b in reads[at : at + 2]]
        tile = []
        for c, i, blocks, to in ((c, i, 2, at),) if (d, j) == (c, i + 1) else ((c, i, 1, at), (d, j, 1, at + 1)):
            zo, own, q, zq, f = parts[c]
            dst = pl.ds(to * LANES, blocks * LANES)
            src = pl.ds(i * LANES, blocks * LANES)
            tile += [
                (zo.at[:, :, src], n_ref.at[:, pl.ds(0, 8), dst]),
                (zq.at[:, :, src], n_ref.at[:, pl.ds(8, 16), dst]),
                (own.at[:, :, src], n_ref.at[:, pl.ds(24, 16), dst]),
                (q.at[:, :, src], n_ref.at[:, pl.ds(40, 16), dst]),
                (f.at[:, pl.ds(foff, 8), src], n_ref.at[:, pl.ds(56, 8), dst]),
            ]
        out.append(tile)
    return out


def kernel(reads, sources, joins, height, width, scal, mix, relcol, *refs):
    n_in = 5 * len(sources)
    parts = {c: refs[5 * i : 5 * i + 5] for i, c in enumerate(sources)}
    g1, g2, g3, bm = refs[n_in : n_in + 4]
    n_in += 4
    if joins:
        earlier = refs[n_in : n_in + len(joins) - 1]
        n_in += len(joins) - 1
    out = refs[n_in]
    n_ref, rr, rc, cv, h1h, h1l, h2h, h2l, h3h, h3l, u_ref, w_ref, sems = refs[n_in + 1 :][:13]
    acc_ref = refs[-1] if joins else out
    blocks = len(reads)
    tiles = blocks // 2
    core, outer, row0, col0 = scal[0], scal[1], scal[2], scal[3]
    foff = pl.multiple_of(core * 8, 8)

    for i, moves in enumerate(copies(reads, foff, parts, n_ref)):
        for src, dst in moves:
            pltpu.make_async_copy(src, dst, sems.at[i]).start()

    i = lax.broadcasted_iota(jnp.int32, (64, 256), 0)
    flipped = jnp.where(i < 8, i + 32, jnp.where(i < 24, i + 8, jnp.where(i < 40, i - 24, jnp.where(i < 56, i - 56, i - 80))))
    row = row0 + jnp.where(core == 0, i - 24, flipped)
    total = window_sum(row, height)
    rr[...] = jnp.where(total > 0.0, 1.0 / jnp.where(total > 0.0, total, 1.0), 0.0)
    col = col0 + relcol[...]
    total = window_sum(col, width)
    rc[...] = jnp.where(total > 0.0, 1.0 / jnp.where(total > 0.0, total, 1.0), 0.0)
    cv[...] = jnp.where((col >= 0) & (col < width), 1.0, 0.0)

    for ref in (h1h, h1l, h2h, h2l, h3h, h3l):
        rows = ref.shape[0]
        ref[:, 0:LANES] = jnp.zeros((rows, LANES), jnp.bfloat16)
        ref[:, pl.ds((blocks + 1) * LANES, 3 * LANES)] = jnp.zeros((rows, 3 * LANES), jnp.bfloat16)

    def tile(j):
        return pl.ds(pl.multiple_of(j * 256, 256), 256)

    def at(j, shift, size):
        return pl.ds(pl.multiple_of(j * 256 + shift, LANES), size)

    def column_pass(high, low, j):
        rows = high.shape[0]
        first = lax.broadcasted_iota(jnp.int32, (rows, LANES), 1) < 64
        mh, ml = high[:, at(j, LANES, 256)], low[:, at(j, LANES, 256)]
        eh = jnp.where(first, high[:, at(j, 3 * LANES, LANES)], high[:, at(j, 0, LANES)])
        el = jnp.where(first, low[:, at(j, 3 * LANES, LANES)], low[:, at(j, 0, LANES)])
        return dot(jnp.concatenate([mh, ml, mh, eh, el, eh], axis=1), bm[...])

    def pipelined(high, low, step):
        rows = high.shape[0]

        def column(j, p):
            u_ref[p, 0:rows, :] = column_pass(high, low, j)

        column(0, 0)

        @pl.loop(0, tiles // 2)
        def _(i):
            column(2 * i + 1, 1)
            step(2 * i, 0)
            column(2 * i + 2, 0)
            step(2 * i + 1, 1)

        if tiles % 2:
            step(tiles - 1, 0)

    def arrived(j):
        window = n_ref.at[:, :, tile(j)]
        pltpu.make_async_copy(window, window, sems.at[j]).wait()

    def first(j):
        scale = rr[...] * rc[0:1, tile(j)]
        for k in range(K):
            hh, hl = row_pass(g1[core], n_ref[k, :, tile(j)] * scale)
            h1h[48 * k : 48 * k + 48, at(j, LANES, 256)] = hh
            h1l[48 * k : 48 * k + 48, at(j, LANES, 256)] = hl

    def stage(j, count):
        for p in range(count):
            arrived(j + p)
        for p in range(count):
            first(j + p)

    @pl.loop(0, tiles // 2)
    def _(j):
        stage(2 * j, 2)

    if tiles % 2:
        stage(tiles - 1, 1)

    def step(j, p):
        acc = jnp.zeros((48, 256), jnp.float32)
        for k in range(K):
            acc = acc + mix[k] * jnp.log(u_ref[p, 48 * k : 48 * k + 48, :])
        valid = cv[0:1, tile(j)] > 0.0
        index = lax.broadcasted_iota(jnp.int32, (48, 256), 0)
        valid = valid & ((index >= 16) | (outer == 0))
        geo = jnp.exp(acc)
        for k in range(K):
            w = jnp.where(valid, geo / u_ref[p, 48 * k : 48 * k + 48, :], 0.0)
            w_ref[k, :, tile(j)] = w[16:32]
            hh, hl = row_pass(g2[core], w)
            h2h[32 * k : 32 * k + 32, at(j, LANES, 256)] = hh
            h2l[32 * k : 32 * k + 32, at(j, LANES, 256)] = hl

    pipelined(h1h, h1l, step)

    zrow = pl.ds(pl.multiple_of(jnp.where(core == 0, 16, 8), 8), 8)
    qrow = pl.ds(pl.multiple_of(jnp.where(core == 0, 40, 48), 8), 8)

    def step(j, p):
        valid = cv[0:1, tile(j)] > 0.0
        for k in range(K):
            n = jnp.concatenate([n_ref[k, zrow, tile(j)], n_ref[k, 24:40, tile(j)], n_ref[k, qrow, tile(j)]], axis=0)
            d = jnp.where(valid, n / u_ref[p, 32 * k : 32 * k + 32, :], 0.0)
            hh, hl = row_pass(g3[core], d)
            h3h[16 * k : 16 * k + 16, at(j, LANES, 256)] = hh
            h3l[16 * k : 16 * k + 16, at(j, LANES, 256)] = hl

    pipelined(h2h, h2l, step)

    def step(j, p):
        acc = jnp.zeros((16, 256), jnp.float32)
        for k in range(K):
            acc = acc + mix[k] * jnp.log(w_ref[k, :, tile(j)] * u_ref[p, 16 * k : 16 * k + 16, :])
        acc_ref[:, tile(j)] = acc

    pipelined(h3h, h3l, step)


    for i, moved in enumerate(joins):
        ref = acc_ref if i == len(joins) - 1 else earlier[i]
        for src, dst, count in moved:
            out[:, dst * LANES : (dst + count) * LANES] = ref[:, src * LANES : (src + count) * LANES]


def relative_columns(reads):
    lane = np.arange(LANES)
    cols = [np.where(lane < 64, 4096 + lane, lane - LANES) if b == EDGE else b * LANES + lane for b in reads]
    return np.tile(np.concatenate(cols).astype(np.int32)[None], (8, 1))


def run_kernel(which, height, width, scal, mix, arrays, earlier):
    reads, sources = KERNELS[which]
    blocks = len(reads)
    lanes = blocks * LANES
    wide = (blocks + 4) * LANES
    consts = matrices()
    smem = pl.BlockSpec(memory_space=pltpu.SMEM)
    vmem = pl.BlockSpec(memory_space=pltpu.VMEM)
    anywhere = pl.BlockSpec(memory_space=pl.ANY)
    scratch = [
        pltpu.VMEM((K, 64, lanes), jnp.float32),
        pltpu.VMEM((64, 256), jnp.float32),
        pltpu.VMEM((8, lanes), jnp.float32),
        pltpu.VMEM((8, lanes), jnp.float32),
    ]
    for rows in (48, 32, 16):
        scratch += [pltpu.VMEM((rows * K, wide), jnp.bfloat16)] * 2
    scratch += [
        pltpu.VMEM((2, 48 * K, 256), jnp.float32),
        pltpu.VMEM((K, 16, lanes), jnp.float32),
        pltpu.SemaphoreType.DMA((blocks // 2,)),
    ]
    in_specs = [smem, smem, vmem] + [anywhere] * len(arrays) + [vmem] * len(consts)
    args = [scal, mix, jnp.asarray(relative_columns(reads)), *arrays, *[jnp.asarray(c) for c in consts]]
    joins = ()
    if earlier:
        joins = tuple(
            tuple((KERNELS[i][0].index(lo), lo, hi - lo + 1) for lo, hi in kept) for i, kept in enumerate(KEPT)
        )
        in_specs += [vmem] * len(earlier)
        args += earlier
        scratch.append(pltpu.VMEM((16, lanes), jnp.float32))
    return pl.pallas_call(
        functools.partial(kernel, reads, sources, joins, height, width),
        out_shape=jax.ShapeDtypeStruct((16, 32 * LANES if earlier else lanes), jnp.float32),
        in_specs=in_specs,
        out_specs=vmem,
        scratch_shapes=scratch,
    )(*args)


def on_device(counts, weights):
    n_rows, n_cols = lax.axis_size("rows"), lax.axis_size("maps")
    height, width = n_rows * counts.shape[1], n_cols * counts.shape[2]
    r, m = lax.axis_index("rows"), lax.axis_index("maps")
    core = r % 2
    outer = ((r == 0) | (r == n_rows - 1)).astype(jnp.int32)
    scal = jnp.stack([core, outer, r * counts.shape[1], m * counts.shape[2]]).astype(jnp.int32)
    mix = lax.optimization_barrier(weights / jnp.sum(weights))

    swap = [(i, i ^ 1) for i in range(n_rows)]
    hop = [(i, i + 2) for i in range(0, n_rows - 2, 2)] + [(i, i - 2) for i in range(3, n_rows, 2)]
    to_right = [(i, i + 1) for i in range(n_cols - 1)]
    to_left = [(i + 1, i) for i in range(n_cols - 1)]

    def after(x, *deps):
        return lax.optimization_barrier((x,) + deps)[0]

    def to_float(x):
        return x.astype(jnp.float32) + 1.0

    def outward(x):
        return lax.dynamic_slice_in_dim(x, (1 - core) * 8, 8, axis=1)

    edge = FIRST * LANES
    zo_own = to_float(outward(counts[..., :edge]))
    zo = [lax.ppermute(zo_own, "rows", hop)]
    n = to_float(after(counts, zo_own))
    left = lax.ppermute(n[..., -LANES:], "maps", to_right)
    right = lax.ppermute(n[..., :LANES], "maps", to_left)
    lane = lax.broadcasted_iota(jnp.int32, left.shape, 2)
    own = [n[..., :edge], jnp.concatenate([n[..., edge:], jnp.where(lane < 64, right, left)], axis=-1)]
    zo.append(lax.ppermute(outward(own[1]), "rows", hop))
    q = [lax.ppermute(x, "rows", swap) for x in own]
    zq = [lax.ppermute(x, "rows", hop) for x in q]
    f = [lax.ppermute(x, "rows", swap) for x in zq]

    def exchange(x, axis, bits):
        size = lax.axis_size(axis)
        got = [lax.ppermute(x, axis, [(d, d ^ bit) for d in range(size)]) for bit in bits]
        return functools.reduce(jnp.add, got, x)

    sums = jnp.sum(n, axis=(1, 2))
    for axis, bits in (
        ("maps", (4,)),
        ("rows", (1,)),
        ("maps", (1,)),
        ("maps", (2,)),
        ("rows", (16, 32, 48)),
        ("rows", (8,)),
        ("rows", (2, 4, 6)),
    ):
        sums = exchange(sums, axis, bits)
    log_scale = jnp.sum(mix * jnp.log(float(height * width) / sums))

    outs = []
    for which in range(len(KERNELS)):
        arrays = []
        for c in KERNELS[which][1]:
            arrays += [zo[c], own[c], q[c], zq[c], f[c]]
        earlier = outs if which == len(KERNELS) - 1 else []
        outs.append(run_kernel(which, height, width, scal, mix, arrays, earlier))
    return jnp.exp(outs[-1] + log_scale)


def solution(mesh):
    return jax.shard_map(
        on_device, mesh=mesh, in_specs=(P(None, "rows", "maps"), P()), out_specs=P("rows", "maps"), check_vma=False
    )
```

```python
import functools

import jax
import jax.numpy as jnp
import numpy as np
from jax import lax
from jax.experimental import pallas as pl
from jax.experimental.pallas import tpu as pltpu
from jax.sharding import PartitionSpec as P


HALF = 8
K = 8
LANES = 128
EDGE = -1

FIRST = 22
CHUNKS = (tuple(range(FIRST)), tuple(range(FIRST, 32)) + (EDGE,))
KERNELS = (
    (tuple(range(FIRST)), (0,)),
    (tuple(range(FIRST - 3, 32)) + (EDGE, 0, 1), (0, 1)),
)
KEPT = (((1, FIRST - 2),), ((FIRST - 1, 31), (0, 0)))


def taps():
    spread = 0.45 * HALF
    a = np.arange(-HALF, HALF + 1, dtype=np.float64)
    g = np.exp(-a * a / (2.0 * spread * spread))
    return g / g.sum()


def band(out_pos, in_pos):
    g = taps()
    d = np.asarray(in_pos)[None, :] - np.asarray(out_pos)[:, None]
    return np.where(np.abs(d) <= HALF, g[np.clip(d + HALF, 0, 2 * HALF)], 0.0)


def split_np(x):
    x = np.asarray(x, np.float32)
    hi = x.astype(jnp.bfloat16)
    lo = (x - hi.astype(np.float32)).astype(jnp.bfloat16)
    return hi, lo


def positions(core):
    own = np.arange(16)
    if core == 0:
        zo, zq, q, f = np.arange(-24, -16), np.arange(-16, 0), np.arange(16, 32), np.arange(32, 40)
        z8, q8 = np.arange(-8, 0), np.arange(16, 24)
    else:
        zo, zq, q, f = np.arange(32, 40), np.arange(16, 32), np.arange(-16, 0), np.arange(-24, -16)
        z8, q8 = np.arange(16, 24), np.arange(-8, 0)
    return np.concatenate([zo, zq, own, q, f]), np.concatenate([zq, own, q]), np.concatenate([z8, own, q8]), own


def matrices():
    out = []
    for s in range(3):
        both = [split_np(band(positions(c)[s + 1], positions(c)[s])) for c in (0, 1)]
        out.append(np.stack([np.concatenate([h, l, h], axis=1) for h, l in both]))
    near = split_np(band(np.arange(256), np.arange(256)).T)
    lane = np.arange(LANES)
    far = split_np(band(np.arange(256), np.where(lane < 64, 256 + lane, lane - LANES)).T)
    out.append(np.concatenate([near[0], near[0], near[1], far[0], far[0], far[1]], axis=0))
    return out


def split(x):
    hi = x.astype(jnp.bfloat16)
    lo = (x - hi.astype(jnp.float32)).astype(jnp.bfloat16)
    return hi, lo


def dot(a, b):
    return jnp.dot(a, b, preferred_element_type=jnp.float32)


def row_pass(g, x):
    hi, lo = split(x)
    return split(dot(g, jnp.concatenate([hi, hi, lo], axis=0)))


def window_sum(pos, size):
    g = taps()
    total = jnp.zeros(pos.shape, jnp.float32)
    for i, a in enumerate(range(-HALF, HALF + 1)):
        total = total + jnp.where((pos + a >= 0) & (pos + a < size), np.float32(g[i]), np.float32(0.0))
    return total


def copies(reads, foff, parts, n_ref):
    where = {b: (c, i) for c, ids in enumerate(CHUNKS) for i, b in enumerate(ids)}
    out = []
    for at in range(0, len(reads), 2):
        (c, i), (d, j) = [where[b] for b in reads[at : at + 2]]
        tile = []
        for c, i, blocks, to in ((c, i, 2, at),) if (d, j) == (c, i + 1) else ((c, i, 1, at), (d, j, 1, at + 1)):
            zo, own, q, zq, f = parts[c]
            dst = pl.ds(to * LANES, blocks * LANES)
            src = pl.ds(i * LANES, blocks * LANES)
            tile += [
                (zo.at[:, :, src], n_ref.at[:, pl.ds(0, 8), dst]),
                (zq.at[:, :, src], n_ref.at[:, pl.ds(8, 16), dst]),
                (own.at[:, :, src], n_ref.at[:, pl.ds(24, 16), dst]),
                (q.at[:, :, src], n_ref.at[:, pl.ds(40, 16), dst]),
                (f.at[:, pl.ds(foff, 8), src], n_ref.at[:, pl.ds(56, 8), dst]),
            ]
        out.append(tile)
    return out


def kernel(reads, sources, joins, height, width, scal, mix, relcol, *refs):
    n_in = 5 * len(sources)
    parts = {c: refs[5 * i : 5 * i + 5] for i, c in enumerate(sources)}
    g1, g2, g3, bm = refs[n_in : n_in + 4]
    n_in += 4
    if joins:
        earlier = refs[n_in : n_in + len(joins) - 1]
        n_in += len(joins) - 1
    out = refs[n_in]
    n_ref, rr, rc, cv, h1h, h1l, h2h, h2l, h3h, h3l, u_ref, w_ref, sems = refs[n_in + 1 :][:13]
    acc_ref = refs[-1] if joins else out
    blocks = len(reads)
    tiles = blocks // 2
    core, outer, row0, col0 = scal[0], scal[1], scal[2], scal[3]
    foff = pl.multiple_of(core * 8, 8)

    for i, moves in enumerate(copies(reads, foff, parts, n_ref)):
        for src, dst in moves:
            pltpu.make_async_copy(src, dst, sems.at[i]).start()

    i = lax.broadcasted_iota(jnp.int32, (64, 256), 0)
    flipped = jnp.where(i < 8, i + 32, jnp.where(i < 24, i + 8, jnp.where(i < 40, i - 24, jnp.where(i < 56, i - 56, i - 80))))
    row = row0 + jnp.where(core == 0, i - 24, flipped)
    total = window_sum(row, height)
    rr[...] = jnp.where(total > 0.0, 1.0 / jnp.where(total > 0.0, total, 1.0), 0.0)
    col = col0 + relcol[...]
    total = window_sum(col, width)
    rc[...] = jnp.where(total > 0.0, 1.0 / jnp.where(total > 0.0, total, 1.0), 0.0)
    cv[...] = jnp.where((col >= 0) & (col < width), 1.0, 0.0)

    for ref in (h1h, h1l, h2h, h2l, h3h, h3l):
        rows = ref.shape[0]
        ref[:, 0:LANES] = jnp.zeros((rows, LANES), jnp.bfloat16)
        ref[:, pl.ds((blocks + 1) * LANES, 3 * LANES)] = jnp.zeros((rows, 3 * LANES), jnp.bfloat16)

    def tile(j):
        return pl.ds(pl.multiple_of(j * 256, 256), 256)

    def at(j, shift, size):
        return pl.ds(pl.multiple_of(j * 256 + shift, LANES), size)

    def column_pass(high, low, j):
        rows = high.shape[0]
        first = lax.broadcasted_iota(jnp.int32, (rows, LANES), 1) < 64
        mh, ml = high[:, at(j, LANES, 256)], low[:, at(j, LANES, 256)]
        eh = jnp.where(first, high[:, at(j, 3 * LANES, LANES)], high[:, at(j, 0, LANES)])
        el = jnp.where(first, low[:, at(j, 3 * LANES, LANES)], low[:, at(j, 0, LANES)])
        return dot(jnp.concatenate([mh, ml, mh, eh, el, eh], axis=1), bm[...])

    def pipelined(high, low, step):
        rows = high.shape[0]

        def column(j, p):
            u_ref[p, 0:rows, :] = column_pass(high, low, j)

        column(0, 0)

        @pl.loop(0, tiles // 2)
        def _(i):
            column(2 * i + 1, 1)
            step(2 * i, 0)
            column(2 * i + 2, 0)
            step(2 * i + 1, 1)

        if tiles % 2:
            step(tiles - 1, 0)

    def arrived(j):
        window = n_ref.at[:, :, tile(j)]
        pltpu.make_async_copy(window, window, sems.at[j]).wait()

    def first(j):
        scale = rr[...] * rc[0:1, tile(j)]
        for k in range(K):
            hh, hl = row_pass(g1[core], n_ref[k, :, tile(j)] * scale)
            h1h[48 * k : 48 * k + 48, at(j, LANES, 256)] = hh
            h1l[48 * k : 48 * k + 48, at(j, LANES, 256)] = hl

    def stage(j, count):
        for p in range(count):
            arrived(j + p)
        for p in range(count):
            first(j + p)

    @pl.loop(0, tiles // 2)
    def _(j):
        stage(2 * j, 2)

    if tiles % 2:
        stage(tiles - 1, 1)

    def step(j, p):
        acc = jnp.zeros((48, 256), jnp.float32)
        for k in range(K):
            acc = acc + mix[k] * jnp.log(u_ref[p, 48 * k : 48 * k + 48, :])
        valid = cv[0:1, tile(j)] > 0.0
        index = lax.broadcasted_iota(jnp.int32, (48, 256), 0)
        valid = valid & ((index >= 16) | (outer == 0))
        geo = jnp.exp(acc)
        for k in range(K):
            w = jnp.where(valid, geo / u_ref[p, 48 * k : 48 * k + 48, :], 0.0)
            w_ref[k, :, tile(j)] = w[16:32]
            hh, hl = row_pass(g2[core], w)
            h2h[32 * k : 32 * k + 32, at(j, LANES, 256)] = hh
            h2l[32 * k : 32 * k + 32, at(j, LANES, 256)] = hl

    pipelined(h1h, h1l, step)

    zrow = pl.ds(pl.multiple_of(jnp.where(core == 0, 16, 8), 8), 8)
    qrow = pl.ds(pl.multiple_of(jnp.where(core == 0, 40, 48), 8), 8)

    def step(j, p):
        valid = cv[0:1, tile(j)] > 0.0
        for k in range(K):
            n = jnp.concatenate([n_ref[k, zrow, tile(j)], n_ref[k, 24:40, tile(j)], n_ref[k, qrow, tile(j)]], axis=0)
            d = jnp.where(valid, n / u_ref[p, 32 * k : 32 * k + 32, :], 0.0)
            hh, hl = row_pass(g3[core], d)
            h3h[16 * k : 16 * k + 16, at(j, LANES, 256)] = hh
            h3l[16 * k : 16 * k + 16, at(j, LANES, 256)] = hl

    pipelined(h2h, h2l, step)

    def step(j, p):
        acc = jnp.zeros((16, 256), jnp.float32)
        for k in range(K):
            acc = acc + mix[k] * jnp.log(w_ref[k, :, tile(j)] * u_ref[p, 16 * k : 16 * k + 16, :])
        acc_ref[:, tile(j)] = acc

    pipelined(h3h, h3l, step)


    for i, moved in enumerate(joins):
        ref = acc_ref if i == len(joins) - 1 else earlier[i]
        for src, dst, count in moved:
            out[:, dst * LANES : (dst + count) * LANES] = ref[:, src * LANES : (src + count) * LANES]


def relative_columns(reads):
    lane = np.arange(LANES)
    cols = [np.where(lane < 64, 4096 + lane, lane - LANES) if b == EDGE else b * LANES + lane for b in reads]
    return np.tile(np.concatenate(cols).astype(np.int32)[None], (8, 1))


def run_kernel(which, height, width, scal, mix, arrays, earlier):
    reads, sources = KERNELS[which]
    blocks = len(reads)
    lanes = blocks * LANES
    wide = (blocks + 4) * LANES
    consts = matrices()
    smem = pl.BlockSpec(memory_space=pltpu.SMEM)
    vmem = pl.BlockSpec(memory_space=pltpu.VMEM)
    anywhere = pl.BlockSpec(memory_space=pl.ANY)
    scratch = [
        pltpu.VMEM((K, 64, lanes), jnp.float32),
        pltpu.VMEM((64, 256), jnp.float32),
        pltpu.VMEM((8, lanes), jnp.float32),
        pltpu.VMEM((8, lanes), jnp.float32),
    ]
    for rows in (48, 32, 16):
        scratch += [pltpu.VMEM((rows * K, wide), jnp.bfloat16)] * 2
    scratch += [
        pltpu.VMEM((2, 48 * K, 256), jnp.float32),
        pltpu.VMEM((K, 16, lanes), jnp.float32),
        pltpu.SemaphoreType.DMA((blocks // 2,)),
    ]
    in_specs = [smem, smem, vmem] + [anywhere] * len(arrays) + [vmem] * len(consts)
    args = [scal, mix, jnp.asarray(relative_columns(reads)), *arrays, *[jnp.asarray(c) for c in consts]]
    joins = ()
    if earlier:
        joins = tuple(
            tuple((KERNELS[i][0].index(lo), lo, hi - lo + 1) for lo, hi in kept) for i, kept in enumerate(KEPT)
        )
        in_specs += [vmem] * len(earlier)
        args += earlier
        scratch.append(pltpu.VMEM((16, lanes), jnp.float32))
    return pl.pallas_call(
        functools.partial(kernel, reads, sources, joins, height, width),
        out_shape=jax.ShapeDtypeStruct((16, 32 * LANES if earlier else lanes), jnp.float32),
        in_specs=in_specs,
        out_specs=vmem,
        scratch_shapes=scratch,
    )(*args)


def on_device(counts, weights):
    n_rows, n_cols = lax.axis_size("rows"), lax.axis_size("maps")
    height, width = n_rows * counts.shape[1], n_cols * counts.shape[2]
    r, m = lax.axis_index("rows"), lax.axis_index("maps")
    core = r % 2
    outer = ((r == 0) | (r == n_rows - 1)).astype(jnp.int32)
    scal = jnp.stack([core, outer, r * counts.shape[1], m * counts.shape[2]]).astype(jnp.int32)
    mix = lax.optimization_barrier(weights / jnp.sum(weights))

    swap = [(i, i ^ 1) for i in range(n_rows)]
    hop = [(i, i + 2) for i in range(0, n_rows - 2, 2)] + [(i, i - 2) for i in range(3, n_rows, 2)]
    to_right = [(i, i + 1) for i in range(n_cols - 1)]
    to_left = [(i + 1, i) for i in range(n_cols - 1)]

    def after(x, *deps):
        return lax.optimization_barrier((x,) + deps)[0]

    def to_float(x):
        return x.astype(jnp.float32) + 1.0

    def outward(x):
        return lax.dynamic_slice_in_dim(x, (1 - core) * 8, 8, axis=1)

    edge = FIRST * LANES
    last, first = to_float(counts[..., -LANES:]), to_float(counts[..., :LANES])
    left = lax.ppermute(last, "maps", to_right)
    right = lax.ppermute(first, "maps", to_left)
    zo_own = to_float(outward(after(counts, last, first)[..., :edge]))
    zo = [lax.ppermute(zo_own, "rows", hop)]
    n = to_float(after(counts, zo_own))
    lane = lax.broadcasted_iota(jnp.int32, left.shape, 2)
    own = [n[..., :edge], jnp.concatenate([n[..., edge:], jnp.where(lane < 64, right, left)], axis=-1)]
    zo.append(lax.ppermute(outward(own[1]), "rows", hop))
    q = [lax.ppermute(x, "rows", swap) for x in own]
    zq = [lax.ppermute(x, "rows", hop) for x in q]
    f = [lax.ppermute(x, "rows", swap) for x in zq]

    def exchange(x, axis, bits):
        size = lax.axis_size(axis)
        got = [lax.ppermute(x, axis, [(d, d ^ bit) for d in range(size)]) for bit in bits]
        return functools.reduce(jnp.add, got, x)

    sums = jnp.sum(n, axis=(1, 2))
    for axis, bits in (
        ("maps", (4,)),
        ("rows", (1,)),
        ("maps", (1,)),
        ("maps", (2,)),
        ("rows", (16, 32, 48)),
        ("rows", (8,)),
        ("rows", (2, 4, 6)),
    ):
        sums = exchange(sums, axis, bits)
    log_scale = jnp.sum(mix * jnp.log(float(height * width) / sums))

    outs = []
    for which in range(len(KERNELS)):
        arrays = []
        for c in KERNELS[which][1]:
            arrays += [zo[c], own[c], q[c], zq[c], f[c]]
        earlier = outs if which == len(KERNELS) - 1 else []
        outs.append(run_kernel(which, height, width, scal, mix, arrays, earlier))
    return jnp.exp(outs[-1] + log_scale)


def solution(mesh):
    return jax.shard_map(
        on_device, mesh=mesh, in_specs=(P(None, "rows", "maps"), P()), out_specs=P("rows", "maps"), check_vma=False
    )
```

```python
import functools

import jax
import jax.numpy as jnp
import numpy as np
from jax import lax
from jax.experimental import pallas as pl
from jax.experimental.pallas import tpu as pltpu
from jax.sharding import PartitionSpec as P


HALF = 8
K = 8
LANES = 128
EDGE = -1

FIRST = 18
CHUNKS = (tuple(range(FIRST)), tuple(range(FIRST, 32)) + (EDGE,))
KERNELS = (
    (tuple(range(FIRST)), (0,)),
    (tuple(range(FIRST - 3, 32)) + (EDGE, 0, 1), (0, 1)),
)
KEPT = (((1, FIRST - 2),), ((FIRST - 1, 31), (0, 0)))


def taps():
    spread = 0.45 * HALF
    a = np.arange(-HALF, HALF + 1, dtype=np.float64)
    g = np.exp(-a * a / (2.0 * spread * spread))
    return g / g.sum()


def band(out_pos, in_pos):
    g = taps()
    d = np.asarray(in_pos)[None, :] - np.asarray(out_pos)[:, None]
    return np.where(np.abs(d) <= HALF, g[np.clip(d + HALF, 0, 2 * HALF)], 0.0)


def split_np(x):
    x = np.asarray(x, np.float32)
    hi = x.astype(jnp.bfloat16)
    lo = (x - hi.astype(np.float32)).astype(jnp.bfloat16)
    return hi, lo


def positions(core):
    own = np.arange(16)
    if core == 0:
        zo, zq, q, f = np.arange(-24, -16), np.arange(-16, 0), np.arange(16, 32), np.arange(32, 40)
        z8, q8 = np.arange(-8, 0), np.arange(16, 24)
    else:
        zo, zq, q, f = np.arange(32, 40), np.arange(16, 32), np.arange(-16, 0), np.arange(-24, -16)
        z8, q8 = np.arange(16, 24), np.arange(-8, 0)
    return np.concatenate([zo, zq, own, q, f]), np.concatenate([zq, own, q]), np.concatenate([z8, own, q8]), own


def matrices():
    out = []
    for s in range(3):
        both = [split_np(band(positions(c)[s + 1], positions(c)[s])) for c in (0, 1)]
        out.append(np.stack([np.concatenate([h, l, h], axis=1) for h, l in both]))
    near = split_np(band(np.arange(256), np.arange(256)).T)
    lane = np.arange(LANES)
    far = split_np(band(np.arange(256), np.where(lane < 64, 256 + lane, lane - LANES)).T)
    out.append(np.concatenate([near[0], near[0], near[1], far[0], far[0], far[1]], axis=0))
    return out


def split(x):
    hi = x.astype(jnp.bfloat16)
    lo = (x - hi.astype(jnp.float32)).astype(jnp.bfloat16)
    return hi, lo


def dot(a, b):
    return jnp.dot(a, b, preferred_element_type=jnp.float32)


def row_pass(g, x):
    hi, lo = split(x)
    return split(dot(g, jnp.concatenate([hi, hi, lo], axis=0)))


def window_sum(pos, size):
    g = taps()
    total = jnp.zeros(pos.shape, jnp.float32)
    for i, a in enumerate(range(-HALF, HALF + 1)):
        total = total + jnp.where((pos + a >= 0) & (pos + a < size), np.float32(g[i]), np.float32(0.0))
    return total


def copies(reads, foff, parts, n_ref):
    where = {b: (c, i) for c, ids in enumerate(CHUNKS) for i, b in enumerate(ids)}
    out = []
    for at in range(0, len(reads), 2):
        (c, i), (d, j) = [where[b] for b in reads[at : at + 2]]
        tile = []
        for c, i, blocks, to in ((c, i, 2, at),) if (d, j) == (c, i + 1) else ((c, i, 1, at), (d, j, 1, at + 1)):
            zo, own, q, zq, f = parts[c]
            dst = pl.ds(to * LANES, blocks * LANES)
            src = pl.ds(i * LANES, blocks * LANES)
            tile += [
                (zo.at[:, :, src], n_ref.at[:, pl.ds(0, 8), dst]),
                (zq.at[:, :, src], n_ref.at[:, pl.ds(8, 16), dst]),
                (own.at[:, :, src], n_ref.at[:, pl.ds(24, 16), dst]),
                (q.at[:, :, src], n_ref.at[:, pl.ds(40, 16), dst]),
                (f.at[:, pl.ds(foff, 8), src], n_ref.at[:, pl.ds(56, 8), dst]),
            ]
        out.append(tile)
    return out


def kernel(reads, sources, joins, height, width, scal, mix, relcol, *refs):
    n_in = 5 * len(sources)
    parts = {c: refs[5 * i : 5 * i + 5] for i, c in enumerate(sources)}
    g1, g2, g3, bm = refs[n_in : n_in + 4]
    n_in += 4
    if joins:
        log_scale, earlier = refs[n_in], refs[n_in + 1 : n_in + len(joins)]
        n_in += len(joins)
    out = refs[n_in]
    n_ref, rr, rc, cv, h1h, h1l, h2h, h2l, h3h, h3l, u_ref, w_ref, sems = refs[n_in + 1 :][:13]
    acc_ref = refs[-1] if joins else out
    blocks = len(reads)
    tiles = blocks // 2
    core, outer, row0, col0 = scal[0], scal[1], scal[2], scal[3]
    foff = pl.multiple_of(core * 8, 8)

    for i, moves in enumerate(copies(reads, foff, parts, n_ref)):
        for src, dst in moves:
            pltpu.make_async_copy(src, dst, sems.at[i]).start()

    i = lax.broadcasted_iota(jnp.int32, (64, 256), 0)
    flipped = jnp.where(i < 8, i + 32, jnp.where(i < 24, i + 8, jnp.where(i < 40, i - 24, jnp.where(i < 56, i - 56, i - 80))))
    row = row0 + jnp.where(core == 0, i - 24, flipped)
    total = window_sum(row, height)
    rr[...] = jnp.where(total > 0.0, 1.0 / jnp.where(total > 0.0, total, 1.0), 0.0)
    col = col0 + relcol[...]
    total = window_sum(col, width)
    rc[...] = jnp.where(total > 0.0, 1.0 / jnp.where(total > 0.0, total, 1.0), 0.0)
    cv[...] = jnp.where((col >= 0) & (col < width), 1.0, 0.0)

    for ref in (h1h, h1l, h2h, h2l, h3h, h3l):
        rows = ref.shape[0]
        ref[:, 0:LANES] = jnp.zeros((rows, LANES), jnp.bfloat16)
        ref[:, pl.ds((blocks + 1) * LANES, 3 * LANES)] = jnp.zeros((rows, 3 * LANES), jnp.bfloat16)

    def tile(j):
        return pl.ds(pl.multiple_of(j * 256, 256), 256)

    def at(j, shift, size):
        return pl.ds(pl.multiple_of(j * 256 + shift, LANES), size)

    def column_pass(high, low, j):
        rows = high.shape[0]
        first = lax.broadcasted_iota(jnp.int32, (rows, LANES), 1) < 64
        mh, ml = high[:, at(j, LANES, 256)], low[:, at(j, LANES, 256)]
        eh = jnp.where(first, high[:, at(j, 3 * LANES, LANES)], high[:, at(j, 0, LANES)])
        el = jnp.where(first, low[:, at(j, 3 * LANES, LANES)], low[:, at(j, 0, LANES)])
        return dot(jnp.concatenate([mh, ml, mh, eh, el, eh], axis=1), bm[...])

    def pipelined(high, low, step):
        rows = high.shape[0]

        def column(j, p):
            u_ref[p, 0:rows, :] = column_pass(high, low, j)

        column(0, 0)

        @pl.loop(0, tiles // 2)
        def _(i):
            column(2 * i + 1, 1)
            step(2 * i, 0)
            column(2 * i + 2, 0)
            step(2 * i + 1, 1)

        if tiles % 2:
            step(tiles - 1, 0)

    def arrived(j):
        window = n_ref.at[:, :, tile(j)]
        pltpu.make_async_copy(window, window, sems.at[j]).wait()

    def first(j):
        scale = rr[...] * rc[0:1, tile(j)]
        for k in range(K):
            hh, hl = row_pass(g1[core], n_ref[k, :, tile(j)] * scale)
            h1h[48 * k : 48 * k + 48, at(j, LANES, 256)] = hh
            h1l[48 * k : 48 * k + 48, at(j, LANES, 256)] = hl

    def stage(j, count):
        for p in range(count):
            arrived(j + p)
        for p in range(count):
            first(j + p)

    @pl.loop(0, tiles // 2)
    def _(j):
        stage(2 * j, 2)

    if tiles % 2:
        stage(tiles - 1, 1)

    def step(j, p):
        acc = jnp.zeros((48, 256), jnp.float32)
        for k in range(K):
            acc = acc + mix[k] * jnp.log(u_ref[p, 48 * k : 48 * k + 48, :])
        valid = cv[0:1, tile(j)] > 0.0
        index = lax.broadcasted_iota(jnp.int32, (48, 256), 0)
        valid = valid & ((index >= 16) | (outer == 0))
        geo = jnp.exp(acc)
        for k in range(K):
            w = jnp.where(valid, geo / u_ref[p, 48 * k : 48 * k + 48, :], 0.0)
            w_ref[k, :, tile(j)] = w[16:32]
            hh, hl = row_pass(g2[core], w)
            h2h[32 * k : 32 * k + 32, at(j, LANES, 256)] = hh
            h2l[32 * k : 32 * k + 32, at(j, LANES, 256)] = hl

    pipelined(h1h, h1l, step)

    zrow = pl.ds(pl.multiple_of(jnp.where(core == 0, 16, 8), 8), 8)
    qrow = pl.ds(pl.multiple_of(jnp.where(core == 0, 40, 48), 8), 8)

    def step(j, p):
        valid = cv[0:1, tile(j)] > 0.0
        for k in range(K):
            n = jnp.concatenate([n_ref[k, zrow, tile(j)], n_ref[k, 24:40, tile(j)], n_ref[k, qrow, tile(j)]], axis=0)
            d = jnp.where(valid, n / u_ref[p, 32 * k : 32 * k + 32, :], 0.0)
            hh, hl = row_pass(g3[core], d)
            h3h[16 * k : 16 * k + 16, at(j, LANES, 256)] = hh
            h3l[16 * k : 16 * k + 16, at(j, LANES, 256)] = hl

    pipelined(h2h, h2l, step)

    def step(j, p):
        acc = jnp.zeros((16, 256), jnp.float32)
        for k in range(K):
            acc = acc + mix[k] * jnp.log(w_ref[k, :, tile(j)] * u_ref[p, 16 * k : 16 * k + 16, :])
        acc_ref[:, tile(j)] = acc

    pipelined(h3h, h3l, step)


    for i, moved in enumerate(joins):
        ref = acc_ref if i == len(joins) - 1 else earlier[i]
        for src, dst, count in moved:
            piece = ref[:, src * LANES : (src + count) * LANES] + log_scale[0]
            out[:, dst * LANES : (dst + count) * LANES] = jnp.exp(piece)


def relative_columns(reads):
    lane = np.arange(LANES)
    cols = [np.where(lane < 64, 4096 + lane, lane - LANES) if b == EDGE else b * LANES + lane for b in reads]
    return np.tile(np.concatenate(cols).astype(np.int32)[None], (8, 1))


def run_kernel(which, height, width, scal, mix, arrays, earlier, log_scale):
    reads, sources = KERNELS[which]
    blocks = len(reads)
    lanes = blocks * LANES
    wide = (blocks + 4) * LANES
    consts = matrices()
    smem = pl.BlockSpec(memory_space=pltpu.SMEM)
    vmem = pl.BlockSpec(memory_space=pltpu.VMEM)
    anywhere = pl.BlockSpec(memory_space=pl.ANY)
    scratch = [
        pltpu.VMEM((K, 64, lanes), jnp.float32),
        pltpu.VMEM((64, 256), jnp.float32),
        pltpu.VMEM((8, lanes), jnp.float32),
        pltpu.VMEM((8, lanes), jnp.float32),
    ]
    for rows in (48, 32, 16):
        scratch += [pltpu.VMEM((rows * K, wide), jnp.bfloat16)] * 2
    scratch += [
        pltpu.VMEM((2, 48 * K, 256), jnp.float32),
        pltpu.VMEM((K, 16, lanes), jnp.float32),
        pltpu.SemaphoreType.DMA((blocks // 2,)),
    ]
    in_specs = [smem, smem, vmem] + [anywhere] * len(arrays) + [vmem] * len(consts)
    args = [scal, mix, jnp.asarray(relative_columns(reads)), *arrays, *[jnp.asarray(c) for c in consts]]
    joins = ()
    if earlier:
        joins = tuple(
            tuple((KERNELS[i][0].index(lo), lo, hi - lo + 1) for lo, hi in kept) for i, kept in enumerate(KEPT)
        )
        in_specs += [smem] + [vmem] * len(earlier)
        args += [log_scale.reshape(1), *earlier]
        scratch.append(pltpu.VMEM((16, lanes), jnp.float32))
    return pl.pallas_call(
        functools.partial(kernel, reads, sources, joins, height, width),
        out_shape=jax.ShapeDtypeStruct((16, 32 * LANES if earlier else lanes), jnp.float32),
        in_specs=in_specs,
        out_specs=vmem,
        scratch_shapes=scratch,
    )(*args)


def on_device(counts, weights):
    n_rows, n_cols = lax.axis_size("rows"), lax.axis_size("maps")
    height, width = n_rows * counts.shape[1], n_cols * counts.shape[2]
    r, m = lax.axis_index("rows"), lax.axis_index("maps")
    core = r % 2
    outer = ((r == 0) | (r == n_rows - 1)).astype(jnp.int32)
    scal = jnp.stack([core, outer, r * counts.shape[1], m * counts.shape[2]]).astype(jnp.int32)
    mix = lax.optimization_barrier(weights / jnp.sum(weights))

    swap = [(i, i ^ 1) for i in range(n_rows)]
    hop = [(i, i + 2) for i in range(0, n_rows - 2, 2)] + [(i, i - 2) for i in range(3, n_rows, 2)]
    to_right = [(i, i + 1) for i in range(n_cols - 1)]
    to_left = [(i + 1, i) for i in range(n_cols - 1)]

    def after(x, *deps):
        return lax.optimization_barrier((x,) + deps)[0]

    def to_float(x):
        return x.astype(jnp.float32) + 1.0

    def outward(x):
        return lax.dynamic_slice_in_dim(x, (1 - core) * 8, 8, axis=1)

    edge = FIRST * LANES
    last, first = to_float(counts[..., -LANES:]), to_float(counts[..., :LANES])
    left = lax.ppermute(last, "maps", to_right)
    right = lax.ppermute(first, "maps", to_left)
    zo_own = to_float(outward(after(counts, last, first)[..., :edge]))
    zo = [lax.ppermute(zo_own, "rows", hop)]
    n = to_float(after(counts, zo_own))
    lane = lax.broadcasted_iota(jnp.int32, left.shape, 2)
    own = [n[..., :edge], jnp.concatenate([n[..., edge:], jnp.where(lane < 64, right, left)], axis=-1)]
    q = [lax.ppermute(x, "rows", swap) for x in own]
    zq = [lax.ppermute(q[0], "rows", hop)]

    axes = ("rows", "maps")
    sums = jnp.sum(n, axis=(1, 2))
    copies_out = after(jnp.broadcast_to(sums, (n_rows * n_cols,) + sums.shape), q[0], own[1])
    everyone = lax.all_to_all(copies_out, axes, 0, 0, tiled=True)
    sums = jnp.sum(everyone, axis=0)
    zo.append(lax.ppermute(outward(own[1]), "rows", hop))
    zq.append(lax.ppermute(q[1], "rows", hop))
    f = [lax.ppermute(x, "rows", swap) for x in zq]
    log_scale = jnp.sum(mix * jnp.log(float(height * width) / sums))

    outs = []
    for which in range(len(KERNELS)):
        arrays = []
        for c in KERNELS[which][1]:
            arrays += [zo[c], own[c], q[c], zq[c], f[c]]
        earlier = outs if which == len(KERNELS) - 1 else []
        outs.append(run_kernel(which, height, width, scal, mix, arrays, earlier, log_scale))
    return outs[-1]


def solution(mesh):
    return jax.shard_map(
        on_device, mesh=mesh, in_specs=(P(None, "rows", "maps"), P()), out_specs=P("rows", "maps"), check_vma=False
    )
```
